32 devices in a mesh: pts: 16 (over z, x, core), modes: 2 (over y).
Axes of the slice: x: 2, y: 2, z: 4, core: 2. Of those that a mesh axis runs over, the one named last changes fastest.
Arguments:
- features: bfloat16 [65536, 128], P('pts'), may hold values from -6 to 6
- coords: float32 [3, 65536], P(None, 'pts'), may hold values from 0 to 1
- quad_weight: float32 [65536], P('pts'), may hold values from 0.5 to 6, as said below
- mode_table: int32 [3, 8192], replicated, may hold values from -8 to 31, as said below
- mode_weight: bfloat16 [8192, 2, 128, 128], P(('pts', 'modes')), may hold values from -4 to 4
- lin_weight: bfloat16 [128, 128], replicated, may hold values from -0.5 to 0.5
- bias: float32 [128], replicated, may hold values from -3 to 3
Outputs:
- output: bfloat16 [65536, 128], P(('pts', 'modes'))
The draws below stay inside these ranges and needn't reach their ends.
Inputs may be any that keep to these rules, and one draw needn't show every extreme that they name: `mode_table`: each column is a distinct triple (kx, ky, kz) with -8 <= kx < 8, -8 <= ky < 8, 0 <= kz < 32; every such triple appears exactly once, in an order drawn from the seed. `quad_weight`: Positive.
All inputs are finite; a program needn't handle non-finite values.
Results may differ from the reference program's by a relative error of at most 0.018.
Values may be sent and summed in bfloat16 or wider, within the bound.
A program may use at most 128 MiB of HBM per device.

```python
import math
import jax
import jax.numpy as jnp
from jax import lax

C = 128
MX = 16
MY = 16
MZ = 32
MODES = 8192
TOTAL = 65536


def draw_quad_weight(key, part):
    ramp = 1.0 + 2.0 * jnp.arange(TOTAL, dtype=jnp.float32) / (TOTAL - 1)
    base = jnp.exp(jax.random.uniform(key, (TOTAL,), jnp.float32, jnp.log(0.5), jnp.log(2.0)))
    return jnp.clip(base * ramp, 0.5, 6.0).astype(jnp.float32)


def draw_mode_table(key, part):
    order = jax.random.permutation(jax.random.fold_in(key, 7), MODES).astype(jnp.int32)
    kx_num = order // (MY * MZ) - MX // 2
    ky_num = order // MZ % MY - MY // 2
    kz_num = order % MZ
    return jnp.stack([kx_num, ky_num, kz_num]).astype(jnp.int32)


def block_scale(stream_key, extent, pieces, low, top_value):
    level, own = 1.0, jax.random.fold_in(stream_key, 6)
    for dim, blocks in pieces:
        draws = jnp.exp(jax.random.uniform(jax.random.fold_in(own, dim), (blocks,), jnp.float32, low / len(pieces), top_value / len(pieces)))
        level = level * jnp.repeat(draws, extent[dim] // blocks).reshape([-1 if axis == dim else 1 for axis in range(len(extent))])
    return level


def gaussian(rng, extent, scale, limit, shards=(), kind=jnp.bfloat16):
    values = scale * jax.random.normal(rng, extent, jnp.float32)
    if shards:
        values = values * block_scale(rng, extent, shards, -0.22, 0.18)
    return jnp.clip(values, -limit, limit).astype(kind)


def setup_inputs(seed: int = 0) -> dict:
    streams_of = jax.random.split(jax.random.key(seed), 8)
    features = gaussian(streams_of[0], (TOTAL, C), 1.0, 6.0, ((0, 16),))
    coords = jnp.clip(1.0 * jax.random.uniform(streams_of[1], (3, TOTAL), jnp.float32) ** block_scale(streams_of[1], (3, TOTAL), ((1, 16),), -0.2, 0.2), 0.0, 1.0)
    quad_weight = draw_quad_weight(jax.random.fold_in(streams_of[7], 71), 0)
    mode_table = draw_mode_table(jax.random.fold_in(streams_of[7], 71), 0)
    mode_weight = gaussian(streams_of[4], (MODES, 2, C, C), ((TOTAL / (MODES * C)) ** 0.5), 4.0, ((0, 32),))
    lin_weight = gaussian(streams_of[5], (C, C), C ** -0.5, 0.5)
    bias = gaussian(streams_of[6], (C,), 0.5, 3.0, (), jnp.float32)
    return {"features": features, "coords": coords, "quad_weight": quad_weight, "mode_table": mode_table, "mode_weight": mode_weight, "lin_weight": lin_weight, "bias": bias}


def phase_basis(coords, wave):
    turns = coords[0][:, None] * wave[0][None, :] + coords[1][:, None] * wave[1][None, :]
    turns = turns + coords[2][:, None] * wave[2][None, :]
    angle = (2.0 * math.pi) * turns
    return jnp.concatenate([jnp.cos(angle), -jnp.sin(angle)], axis=1).astype(jnp.bfloat16)


def reference(features, coords, quad_weight, mode_table, mode_weight, lin_weight, bias):
    weighted = (quad_weight[:, None] * features.astype(jnp.float32)).astype(jnp.bfloat16)
    total = jnp.sum(quad_weight)
    wave = mode_table.astype(jnp.float32)
    blocks = MODES // 256
    wave_blocks = wave.reshape(3, blocks, 256).transpose(1, 0, 2)
    weighted_f = weighted.astype(jnp.float32)

    def analyse(part_wave):
        basis = phase_basis(coords, part_wave).astype(jnp.float32)
        res = lax.dot_general(basis, weighted_f, (((0,), (0,)), ((), ())), preferred_element_type=jnp.float32)
        return res.reshape(2, 256, C).transpose(1, 0, 2).reshape(256, 2 * C)

    coef = lax.map(analyse, wave_blocks).reshape(MODES, 2 * C).astype(jnp.bfloat16)
    real_in = coef[:, :C].astype(jnp.float32)
    imag_in = coef[:, C:].astype(jnp.float32)
    w_real = mode_weight[:, 0].astype(jnp.float32)
    w_imag = mode_weight[:, 1].astype(jnp.float32)
    real_out = jnp.einsum("mc,mcd->md", real_in, w_real) - jnp.einsum("mc,mcd->md", imag_in, w_imag)
    imag_out = jnp.einsum("mc,mcd->md", real_in, w_imag) + jnp.einsum("mc,mcd->md", imag_in, w_real)
    filtered = jnp.concatenate([real_out, imag_out], axis=1).astype(jnp.bfloat16)
    filt_blocks = filtered.reshape(blocks, 256, 2 * C)

    def synthesize(carry, inputs):
        part_wave, piece = inputs
        basis = phase_basis(coords, part_wave).astype(jnp.float32)
        rhs = jnp.concatenate([piece[:, :C], piece[:, C:]], axis=0).astype(jnp.float32)
        return carry + jnp.dot(basis, rhs, preferred_element_type=jnp.float32), None

    spectral, unused = lax.scan(synthesize, jnp.zeros((TOTAL, C), jnp.float32), (wave_blocks, filt_blocks))
    linear = jnp.dot(features, lin_weight, preferred_element_type=jnp.float32)
    pre = spectral / total + linear + bias[None, :]
    return jax.nn.gelu(pre, approximate=False).astype(jnp.bfloat16)
```

```python
import functools
import math

import jax
import jax.numpy as jnp
from jax import lax
from jax.experimental import pallas as pl
from jax.experimental.pallas import tpu as pltpu
from jax.sharding import Mesh
from jax.sharding import PartitionSpec as P

KX_LOW, KX_COUNT = -8, 16
KY_LOW, KY_COUNT = -8, 16
KZ_LOW, KZ_COUNT = 0, 32
HALF = KX_COUNT // 2
PLANE = KY_COUNT * KZ_COUNT
PTS = ("z", "x", "core")
AXES = PTS + ("modes",)


def cos_sin(turns):
    angle = (2.0 * math.pi) * (turns - jnp.round(turns))
    return jnp.cos(angle), jnp.sin(angle)


def factors(coords):
    x, y, z = coords[0], coords[1], coords[2]
    j = jnp.arange(HALF, dtype=jnp.float32) + 0.5
    xc, xs = cos_sin(j[:, None] * x[None, :])
    ky = jnp.arange(KY_COUNT, dtype=jnp.float32) + KY_LOW
    kz = jnp.arange(KZ_COUNT, dtype=jnp.float32) + KZ_LOW
    yc, ys = cos_sin(ky[:, None] * y[None, :])
    zc, zs = cos_sin(kz[:, None] * z[None, :] - 0.5 * x[None, :])
    return jnp.concatenate([xc, xs], axis=0).T, (yc, ys, zc, zs)


def plane_kernel(yc_ref, ys_ref, zc_ref, zs_ref, e_ref, et_ref):
    zc, zs = zc_ref[...], zs_ref[...]
    for k in range(KY_COUNT):
        yc, ys = yc_ref[pl.ds(k, 1)], ys_ref[pl.ds(k, 1)]
        re = yc * zc - ys * zs
        im = ys * zc + yc * zs
        e_ref[pl.ds(k * KZ_COUNT, KZ_COUNT)] = re.astype(jnp.bfloat16)
        e_ref[pl.ds(PLANE + k * KZ_COUNT, KZ_COUNT)] = im.astype(jnp.bfloat16)
    et_ref[...] = e_ref[...].T


def plane_factors(parts):
    rows = parts[0].shape[1]
    step = math.gcd(rows, 512)
    return pl.pallas_call(
        plane_kernel,
        grid=(rows // step,),
        out_shape=(
            jax.ShapeDtypeStruct((2 * PLANE, rows), jnp.bfloat16),
            jax.ShapeDtypeStruct((rows, 2 * PLANE), jnp.bfloat16),
        ),
        in_specs=[pl.BlockSpec((part.shape[0], step), lambda p: (0, p)) for part in parts],
        out_specs=(
            pl.BlockSpec((2 * PLANE, step), lambda p: (0, p)),
            pl.BlockSpec((step, 2 * PLANE), lambda p: (p, 0)),
        ),
        compiler_params=pltpu.CompilerParams(vmem_limit_bytes=48 << 20),
    )(*parts)


def column(table_ref, at):
    lanes = lax.broadcasted_iota(jnp.int32, table_ref.shape, 1)
    return jnp.sum(jnp.where(lanes == at, table_ref[...], 0.0), axis=1, keepdims=True)


def analyse_kernel(e_ref, xf_ref, weighted_ref, out_ref):
    j = pl.program_id(0)
    width = weighted_ref.shape[1]
    weighted = weighted_ref[...].astype(jnp.float32)
    by_cos = (column(xf_ref, j) * weighted).astype(jnp.bfloat16)
    by_sin = (column(xf_ref, HALF + j) * weighted).astype(jnp.bfloat16)
    rhs = jnp.concatenate([by_cos, by_sin], axis=1)
    re = jnp.dot(e_ref[:PLANE], rhs, preferred_element_type=jnp.float32)
    im = jnp.dot(e_ref[PLANE:], rhs, preferred_element_type=jnp.float32)
    rc, rs = re[:, :width], re[:, width:]
    ic, is_ = im[:, :width], im[:, width:]
    out_ref[0, 0, :, :width] = (rc - is_).astype(jnp.bfloat16)
    out_ref[0, 0, :, width:] = (-(ic + rs)).astype(jnp.bfloat16)
    out_ref[1, 0, :, :width] = (rc + is_).astype(jnp.bfloat16)
    out_ref[1, 0, :, width:] = (rs - ic).astype(jnp.bfloat16)


def analyse(e, xf, weighted):
    rows, width = weighted.shape
    out = pl.pallas_call(
        analyse_kernel,
        grid=(HALF,),
        out_shape=jax.ShapeDtypeStruct((2, HALF, PLANE, 2 * width), jnp.bfloat16),
        in_specs=[
            pl.BlockSpec((2 * PLANE, rows), lambda j: (0, 0)),
            pl.BlockSpec((rows, 2 * HALF), lambda j: (0, 0)),
            pl.BlockSpec((rows, width), lambda j: (0, 0)),
        ],
        out_specs=pl.BlockSpec((2, 1, PLANE, 2 * width), lambda j: (0, j, 0, 0)),
        compiler_params=pltpu.CompilerParams(vmem_limit_bytes=48 << 20),
    )(e, xf, weighted)
    return out.reshape(2 * HALF * PLANE, 2 * width)


def synthesize_kernel(et_ref, xf_ref, full_ref, out_ref):
    j = pl.program_id(0)
    width = out_ref.shape[1]
    pos = full_ref[0, 0].astype(jnp.float32)
    neg = full_ref[1, 0].astype(jnp.float32)
    pr, pi = pos[:, :width], pos[:, width:]
    nr, ni = neg[:, :width], neg[:, width:]
    top = jnp.concatenate([pr + nr, ni - pi], axis=1).astype(jnp.bfloat16)
    low = jnp.concatenate([-(pi + ni), nr - pr], axis=1).astype(jnp.bfloat16)
    field = jnp.dot(et_ref[:, :PLANE], top, preferred_element_type=jnp.float32)
    field = field + jnp.dot(et_ref[:, PLANE:], low, preferred_element_type=jnp.float32)
    add = column(xf_ref, j) * field[:, :width] + column(xf_ref, HALF + j) * field[:, width:]

    @pl.when(j == 0)
    def _():
        out_ref[...] = add

    @pl.when(j > 0)
    def _():
        out_ref[...] += add


def synthesize(et, xf, full):
    rows = et.shape[0]
    width = full.shape[1] // 2
    return pl.pallas_call(
        synthesize_kernel,
        grid=(HALF,),
        out_shape=jax.ShapeDtypeStruct((rows, width), jnp.float32),
        in_specs=[
            pl.BlockSpec((rows, 2 * PLANE), lambda j: (0, 0)),
            pl.BlockSpec((rows, 2 * HALF), lambda j: (0, 0)),
            pl.BlockSpec((2, 1, PLANE, 2 * width), lambda j: (0, j, 0, 0)),
        ],
        out_specs=pl.BlockSpec((rows, width), lambda j: (0, 0)),
        compiler_params=pltpu.CompilerParams(vmem_limit_bytes=48 << 20),
    )(et, xf, full.reshape(2, HALF, PLANE, 2 * width))


def exchange_kernel(sizes, coef_ref, weight_ref, out_ref, w_ref, came0, came1, came2, came3, sum1, sum2, sum3, w_sem, sends, recvs):
    n_x, n_y, n_z = sizes
    chunks, rows, wide = coef_ref.shape[1], coef_ref.shape[3], coef_ref.shape[4]
    width = wide // 2
    x, y, z = (lax.axis_index(a) for a in ("x", "modes", "z"))
    core = lax.axis_index("core")
    f32 = jnp.float32
    bf16 = jnp.bfloat16

    loads = []
    for k in range(chunks):
        part = pl.ds(k * rows, rows)
        loads.append(pltpu.make_async_copy(weight_ref.at[part], w_ref.at[part], w_sem.at[k]))
        loads[-1].start()

    peers = [{"core": 1 - core}]
    for axis, at, n in (("x", x, n_x), ("modes", y, n_y), ("z", z, n_z)):
        peers += [{axis: lax.rem(at + o, n)} for o in range(1, n)]
    barrier = pltpu.get_barrier_semaphore()
    for peer in peers:
        pl.semaphore_signal(barrier, inc=1, device_id=peer, device_id_type=pl.DeviceIdType.MESH)
    pl.semaphore_wait(barrier, len(peers))

    started = []

    def send(stage, k, o, src, dst, peer):
        copy = pltpu.make_async_remote_copy(
            src_ref=src,
            dst_ref=dst,
            send_sem=sends.at[stage, k, o - 1],
            recv_sem=recvs.at[stage, k, o - 1],
            device_id=peer,
            device_id_type=pl.DeviceIdType.MESH,
        )
        copy.start()
        started.append(copy)
        return copy

    def plan(k):
        if k % 2 == 0:
            return ("x", x, n_x), ("modes", y, n_y)
        return ("modes", y, n_y), ("x", x, n_x)

    def partial(k, base, count, level):
        (_, at1, n1), (_, at2, n2) = plan(k)
        total = coef_ref[core, k, pl.ds(base, count)].astype(f32) + came0[k, pl.ds(base, count)].astype(f32)
        if level >= 1:
            inner = base - at1 * (n2 * n_z)
            for o in range(n1 - 1):
                total += came1[k, pl.ds(o * n2 * n_z + inner, count)].astype(f32)
        if level >= 2:
            inner = inner - at2 * n_z
            for o in range(n2 - 1):
                total += came2[k, pl.ds(o * n_z + inner, count)].astype(f32)
        return total

    got = {}

    def scatter1(k):
        got[0, k][0].wait_recv()
        (axis, at, n), (_, _, n2) = plan(k)
        count = n2 * n_z
        copies = []
        for o in range(1, n):
            to = lax.rem(at + o, n)
            slot = pl.ds((o - 1) * count, count)
            sum1[k, slot] = partial(k, to * count, count, 0).astype(bf16)
            copies.append(send(1, k, o, sum1.at[k, slot], came1.at[k, slot], {axis: to}))
        got[1, k] = copies

    def scatter2(k):
        for copy in got[1, k]:
            copy.wait_recv()
        (_, at1, _), (axis, at, n) = plan(k)
        copies = []
        for o in range(1, n):
            to = lax.rem(at + o, n)
            slot = pl.ds((o - 1) * n_z, n_z)
            sum2[k, slot] = partial(k, (at1 * n + to) * n_z, n_z, 1).astype(bf16)
            copies.append(send(2, k, o, sum2.at[k, slot], came2.at[k, slot], {axis: to}))
        got[2, k] = copies

    def own_base(k):
        (_, at1, _), (_, at2, n2) = plan(k)
        return (at1 * n2 + at2) * n_z

    def scatter3(k):
        for copy in got[2, k]:
            copy.wait_recv()
        copies = []
        for o in range(1, n_z):
            to = lax.rem(z + o, n_z)
            slot = pl.ds(o - 1, 1)
            sum3[k, slot] = partial(k, own_base(k) + to, 1, 2).astype(bf16)
            copies.append(send(3, k, o, sum3.at[k, slot], came3.at[k, slot], {"z": to}))
        got[3, k] = copies

    def mix(k):
        for copy in got[3, k]:
            copy.wait_recv()
        total = partial(k, own_base(k) + z, 1, 2)[0]
        for o in range(n_z - 1):
            total += came3[k, o].astype(f32)
        coef = total.astype(bf16)
        re, im = coef[:, :width], coef[:, width:]
        lhs = jnp.concatenate(
            [jnp.concatenate([re, -im], axis=1), jnp.concatenate([im, re], axis=1)], axis=0
        )
        ids = lax.rem(lax.broadcasted_iota(jnp.int32, (2 * rows, width), 0), rows)
        loads[k].wait()
        unroll = 4

        def body(step, acc):
            for i in range(unroll):
                m = step * unroll + i
                w = w_ref[k * rows + m].reshape(2 * width, width)
                res = jnp.dot(lhs, w, preferred_element_type=f32)
                acc = jnp.where(ids == m, res, acc)
            return acc

        acc = lax.fori_loop(0, rows // unroll, body, jnp.zeros((2 * rows, width), f32))
        block = own_base(k) + z
        out_ref[core, k, block, :, :width] = acc[:rows].astype(bf16)
        out_ref[core, k, block, :, width:] = acc[rows:].astype(bf16)
        where = out_ref.at[core, k, block]
        got[4, k] = [send(4, k, o, where, where, {"z": lax.rem(z + o, n_z)}) for o in range(1, n_z)]

    def gather2(k):
        for copy in got[4, k]:
            copy.wait_recv()
        _, (axis, at, n) = plan(k)
        where = out_ref.at[core, k, pl.ds(own_base(k), n_z)]
        got[5, k] = [send(5, k, o, where, where, {axis: lax.rem(at + o, n)}) for o in range(1, n)]

    def gather1(k):
        for copy in got[5, k]:
            copy.wait_recv()
        (axis, at, n), (_, _, n2) = plan(k)
        count = n2 * n_z
        where = out_ref.at[core, k, pl.ds(at * count, count)]
        got[6, k] = [send(6, k, o, where, where, {axis: lax.rem(at + o, n)}) for o in range(1, n)]

    def gather0(k):
        for copy in got[6, k]:
            copy.wait_recv()
        where = out_ref.at[core, k]
        got[7, k] = [send(7, k, 1, where, where, {"core": 1 - core})]

    for k in range(chunks):
        got[0, k] = [send(0, k, 1, coef_ref.at[1 - core, k], came0.at[k], {"core": 1 - core})]
    for k in range(chunks):
        scatter1(k)
    stages = [scatter2, scatter3, mix, gather2, gather1, gather0]
    for t in range(chunks + len(stages) - 1):
        for s in reversed(range(len(stages))):
            if 0 <= t - s < chunks:
                stages[s](t - s)
    for k in range(chunks):
        got[7, k][0].wait_recv()
    for copy in started:
        copy.wait_send()


def exchange(coef, weight, sizes):
    n_x, n_y, n_z = sizes
    _, chunks, blocks, rows, wide = coef.shape
    width = wide // 2
    one = max((n_x - 1) * n_y, (n_y - 1) * n_x) * n_z
    two = max(n_x - 1, n_y - 1) * n_z
    three = max(n_z - 1, 1)
    hops = max(n_x, n_y, n_z, 2) - 1

    def buf(n):
        return pltpu.VMEM((chunks, n, rows, wide), jnp.bfloat16)

    return pl.pallas_call(
        functools.partial(exchange_kernel, sizes),
        out_shape=jax.ShapeDtypeStruct(coef.shape, jnp.bfloat16),
        in_specs=[pl.BlockSpec(memory_space=pltpu.VMEM), pl.BlockSpec(memory_space=pl.ANY)],
        out_specs=pl.BlockSpec(memory_space=pltpu.VMEM),
        scratch_shapes=[
            pltpu.VMEM(weight.shape, jnp.bfloat16),
            buf(blocks), buf(one), buf(two), buf(three), buf(one), buf(two), buf(three),
            pltpu.SemaphoreType.DMA((chunks,)),
            pltpu.SemaphoreType.DMA((8, chunks, hops)),
            pltpu.SemaphoreType.DMA((8, chunks, hops)),
        ],
        compiler_params=pltpu.CompilerParams(
            collective_id=0, has_side_effects=True, vmem_limit_bytes=48 << 20
        ),
    )(coef, weight)


def chunk_rows(own):
    chunks = max(2, min(8, own // 16))
    return chunks, own // chunks


def to_layout(values, sizes, own):
    n_x, n_y, n_z = sizes
    chunks, rows = chunk_rows(own)
    v = values.reshape(n_z, n_x, 2, n_y, chunks // 2, 2, rows)
    even = v[:, :, :, :, :, 0].transpose(2, 4, 1, 3, 0, 5).reshape(2, chunks // 2, -1)
    odd = v[:, :, :, :, :, 1].transpose(2, 4, 3, 1, 0, 5).reshape(2, chunks // 2, -1)
    return jnp.stack([even, odd], axis=2).reshape(-1)


def place_of(mode, sizes, own):
    n_x, n_y, n_z = sizes
    chunks, rows = chunk_rows(own)
    device, row = mode // own, mode % own
    y, pair = device % n_y, device // n_y
    core, chip = pair % 2, pair // 2
    x, z = chip % n_x, chip // n_x
    k = row // rows
    block = jnp.where(k % 2 == 0, x * n_y + y, y * n_x + x) * n_z + z
    return ((core * chunks + k) * (n_x * n_y * n_z) + block) * rows + row % rows


def take_kernel(index_ref, *refs):
    *src_refs, out_ref, wide, picked = refs

    @pl.when(pl.program_id(0) == 0)
    def _():
        for i, src_ref in enumerate(src_refs):
            n = src_ref.shape[0]
            wide[i * n : (i + 1) * n] = src_ref[...].astype(jnp.float32)

    rows = out_ref.shape[0]
    base = pl.program_id(0) * rows
    unroll = math.gcd(rows, 32)

    def body(block, carry):
        at = block * unroll
        sources = [index_ref[base + at + k] for k in range(unroll)]
        found = [wide[pl.ds(source, 1), :] for source in sources]
        start = pl.multiple_of(at, unroll)
        picked[pl.ds(start, unroll), :] = jnp.concatenate(found, axis=0)
        return carry

    lax.fori_loop(0, rows // unroll, body, 0)
    out_ref[...] = picked[...].astype(out_ref.dtype)


def take_rows(tables, index):
    n, width = tables[0].shape
    m = index.shape[0]
    step = math.gcd(m, 512)
    return pl.pallas_call(
        take_kernel,
        out_shape=jax.ShapeDtypeStruct((m, width), tables[0].dtype),
        grid_spec=pltpu.PrefetchScalarGridSpec(
            num_scalar_prefetch=1,
            grid=(m // step,),
            in_specs=[pl.BlockSpec((n, width), lambda b, index: (0, 0)) for _ in tables],
            out_specs=pl.BlockSpec((step, width), lambda b, index: (b, 0)),
            scratch_shapes=[
                pltpu.VMEM((len(tables) * n, width), jnp.float32),
                pltpu.VMEM((step, width), jnp.float32),
            ],
        ),
        compiler_params=pltpu.CompilerParams(vmem_limit_bytes=48 << 20),
    )(index, *tables)


def grid_index(mode_table):
    kx = mode_table[0]
    slot = jnp.where(kx >= 0, kx, HALF - 1 - kx)
    return (slot * KY_COUNT + mode_table[1] - KY_LOW) * KZ_COUNT + mode_table[2] - KZ_LOW


def inverse_index(index):
    n = index.shape[0]
    lo = 128
    hi = n // lo
    ids = jnp.arange(n, dtype=jnp.int32)
    hot_lo = (index[:, None] % lo == jnp.arange(lo)[None, :]).astype(jnp.bfloat16)
    hit = index[None, :] // lo == jnp.arange(hi)[:, None]
    top = jnp.where(hit, ids[None, :] // lo, 0).astype(jnp.bfloat16)
    low = jnp.where(hit, ids[None, :] % lo, 0).astype(jnp.bfloat16)
    got = jnp.dot(jnp.concatenate([top, low], axis=0), hot_lo, preferred_element_type=jnp.float32)
    return (got[:hi] * lo + got[hi:]).astype(jnp.int32).reshape(n)


def on_device(features, coords, quad_weight, mode_table, mode_weight, lin_weight, bias):
    width = features.shape[1]
    sizes = tuple(lax.axis_size(a) for a in ("x", "modes", "z"))
    group = lax.axis_index("modes")
    rows = features.shape[0] // sizes[1]
    features = lax.dynamic_slice_in_dim(features, group * rows, rows, 0)
    coords = lax.dynamic_slice_in_dim(coords, group * rows, rows, 1)
    quad = lax.dynamic_slice_in_dim(quad_weight, group * rows, rows, 0)
    own = mode_weight.shape[0]
    total = lax.psum(jnp.sum(quad), AXES)
    xf, parts = factors(coords)
    e, et = plane_factors(parts)
    index = grid_index(mode_table)
    inverse = inverse_index(index)
    weighted = (quad[:, None] * features.astype(jnp.float32)).astype(jnp.bfloat16)
    coef = analyse(e, xf, weighted)
    coef = take_rows([coef], to_layout(index, sizes, own))
    chunks, step = chunk_rows(own)
    full = exchange(coef.reshape(2, chunks, -1, step, 2 * width), mode_weight, sizes)
    full = take_rows([full.reshape(-1, 2 * width)], place_of(inverse, sizes, own))
    spectral = synthesize(et, xf, full)
    linear = jnp.dot(features, lin_weight, preferred_element_type=jnp.float32)
    pre = spectral / total + linear + bias[None, :]
    return jax.nn.gelu(pre, approximate=False).astype(jnp.bfloat16)


def solution(mesh):
    chips = mesh.shape["pts"] // 2
    n_x = 2 if chips % 2 == 0 else 1
    shape = (chips // n_x, n_x, 2, mesh.shape["modes"])
    mesh = Mesh(mesh.devices.reshape(shape), AXES)
    return jax.shard_map(
        on_device,
        mesh=mesh,
        in_specs=(
            P(PTS, None),
            P(None, PTS),
            P(PTS),
            P(),
            P(AXES, None, None, None),
            P(),
            P(),
        ),
        out_specs=P(AXES, None),
        check_vma=False,
    )
```

```python
import functools
import math

import jax
import jax.numpy as jnp
from jax import lax
from jax.experimental import pallas as pl
from jax.experimental.pallas import tpu as pltpu
from jax.sharding import Mesh
from jax.sharding import PartitionSpec as P

KX_LOW, KX_COUNT = -8, 16
KY_LOW, KY_COUNT = -8, 16
KZ_LOW, KZ_COUNT = 0, 32
HALF = KX_COUNT // 2
PLANE = KY_COUNT * KZ_COUNT
PTS = ("z", "x", "core")
AXES = PTS + ("modes",)


def cos_sin(turns):
    angle = (2.0 * math.pi) * (turns - jnp.round(turns))
    return jnp.cos(angle), jnp.sin(angle)


def factors(coords):
    x, y, z = coords[0], coords[1], coords[2]
    j = jnp.arange(HALF, dtype=jnp.float32) + 0.5
    xc, xs = cos_sin(j[:, None] * x[None, :])
    ky = jnp.arange(KY_COUNT, dtype=jnp.float32) + KY_LOW
    kz = jnp.arange(KZ_COUNT, dtype=jnp.float32) + KZ_LOW
    yc, ys = cos_sin(ky[:, None] * y[None, :])
    zc, zs = cos_sin(kz[:, None] * z[None, :] - 0.5 * x[None, :])
    return xc, xs, (yc, ys, zc, zs)


def plane_kernel(yc_ref, ys_ref, zc_ref, zs_ref, e_ref, et_ref):
    zc, zs = zc_ref[...], zs_ref[...]
    for k in range(KY_COUNT):
        yc, ys = yc_ref[pl.ds(k, 1)], ys_ref[pl.ds(k, 1)]
        re = yc * zc - ys * zs
        im = ys * zc + yc * zs
        e_ref[pl.ds(k * KZ_COUNT, KZ_COUNT)] = re.astype(jnp.bfloat16)
        e_ref[pl.ds(PLANE + k * KZ_COUNT, KZ_COUNT)] = im.astype(jnp.bfloat16)
    et_ref[...] = e_ref[...].T


def plane_factors(parts):
    rows = parts[0].shape[1]
    step = math.gcd(rows, 512)
    return pl.pallas_call(
        plane_kernel,
        grid=(rows // step,),
        out_shape=(
            jax.ShapeDtypeStruct((2 * PLANE, rows), jnp.bfloat16),
            jax.ShapeDtypeStruct((rows, 2 * PLANE), jnp.bfloat16),
        ),
        in_specs=[pl.BlockSpec((part.shape[0], step), lambda p: (0, p)) for part in parts],
        out_specs=(
            pl.BlockSpec((2 * PLANE, step), lambda p: (0, p)),
            pl.BlockSpec((step, 2 * PLANE), lambda p: (p, 0)),
        ),
        compiler_params=pltpu.CompilerParams(vmem_limit_bytes=48 << 20),
    )(*parts)


def row_loop(count, unroll, body):
    def step(block, carry):
        for i in range(unroll):
            body(block * unroll + i)
        return carry

    lax.fori_loop(0, count // unroll, step, 0)


def analyse_kernel(place_ref, e_ref, xt_ref, weighted_ref, out_ref, re_tab, im_tab, stage):
    j = pl.program_id(0)
    width = weighted_ref.shape[0]
    weighted = weighted_ref[...]
    by_cos = (xt_ref[pl.ds(j, 1)] * weighted).astype(jnp.bfloat16)
    by_sin = (xt_ref[pl.ds(HALF + j, 1)] * weighted).astype(jnp.bfloat16)
    rhs = jnp.concatenate([by_cos, by_sin], axis=0)
    dims = (((1,), (1,)), ((), ()))
    re = lax.dot_general(e_ref[:PLANE], rhs, dims, preferred_element_type=jnp.float32)
    im = lax.dot_general(e_ref[PLANE:], rhs, dims, preferred_element_type=jnp.float32)
    rc, rs = re[:, :width], re[:, width:]
    ic, is_ = im[:, :width], im[:, width:]
    stage[0] = rc - is_
    stage[1] = -(ic + rs)
    stage[2] = rc + is_
    stage[3] = rs - ic

    def move(q):
        for half in range(2):
            to = pl.ds(place_ref[(half * HALF + j) * PLANE + q], 1)
            re_tab[to] = stage[2 * half, pl.ds(q, 1)]
            im_tab[to] = stage[2 * half + 1, pl.ds(q, 1)]

    row_loop(PLANE, 16, move)

    @pl.when(j == pl.num_programs(0) - 1)
    def _():
        n = 256

        def body(i, carry):
            at = pl.ds(pl.multiple_of(i * n, n), n)
            out_ref[at, :width] = re_tab[at].astype(jnp.bfloat16)
            out_ref[at, width:] = im_tab[at].astype(jnp.bfloat16)
            return carry

        lax.fori_loop(0, out_ref.shape[0] // n, body, 0)


def analyse(place, e, xt, weighted):
    width, rows = weighted.shape
    modes = 2 * HALF * PLANE
    return pl.pallas_call(
        analyse_kernel,
        out_shape=jax.ShapeDtypeStruct((modes, 2 * width), jnp.bfloat16),
        grid_spec=pltpu.PrefetchScalarGridSpec(
            num_scalar_prefetch=1,
            grid=(HALF,),
            in_specs=[
                pl.BlockSpec((2 * PLANE, rows), lambda j, place: (0, 0)),
                pl.BlockSpec((2 * HALF, rows), lambda j, place: (0, 0)),
                pl.BlockSpec((width, rows), lambda j, place: (0, 0)),
            ],
            out_specs=pl.BlockSpec((modes, 2 * width), lambda j, place: (0, 0)),
            scratch_shapes=[
                pltpu.VMEM((modes, width), jnp.float32),
                pltpu.VMEM((modes, width), jnp.float32),
                pltpu.VMEM((4, PLANE, width), jnp.float32),
            ],
        ),
        compiler_params=pltpu.CompilerParams(vmem_limit_bytes=48 << 20),
    )(place, e, xt, weighted)


def synthesize_kernel(
    place_ref, et_ref, xf_ref, full_ref, features_ref, lin_ref, bias_ref, total_ref, out_ref, re_tab, im_tab, stage, acc_ref
):
    j = pl.program_id(0)
    width = out_ref.shape[1]
    f32 = jnp.float32

    @pl.when(j == 0)
    def _():
        n = 256

        def body(i, carry):
            at = pl.ds(pl.multiple_of(i * n, n), n)
            re_tab[at] = full_ref[at, :width].astype(f32)
            im_tab[at] = full_ref[at, width:].astype(f32)
            return carry

        lax.fori_loop(0, full_ref.shape[0] // n, body, 0)

    def move(q):
        for half in range(2):
            at = pl.ds(place_ref[(half * HALF + j) * PLANE + q], 1)
            stage[2 * half, pl.ds(q, 1)] = re_tab[at]
            stage[2 * half + 1, pl.ds(q, 1)] = im_tab[at]

    row_loop(PLANE, 16, move)
    pr, pi, nr, ni = stage[0], stage[1], stage[2], stage[3]
    top = jnp.concatenate([pr + nr, ni - pi], axis=1).astype(jnp.bfloat16)
    low = jnp.concatenate([-(pi + ni), nr - pr], axis=1).astype(jnp.bfloat16)
    field = jnp.dot(et_ref[:, :PLANE], top, preferred_element_type=f32)
    field = field + jnp.dot(et_ref[:, PLANE:], low, preferred_element_type=f32)
    add = xf_ref[0, :, 0:1] * field[:, :width] + xf_ref[0, :, 1:2] * field[:, width:]

    @pl.when(j == 0)
    def _():
        acc_ref[...] = add

    @pl.when(j > 0)
    def _():
        acc_ref[...] += add

    @pl.when(j == pl.num_programs(0) - 1)
    def _():
        linear = jnp.dot(features_ref[...], lin_ref[...], preferred_element_type=f32)
        pre = acc_ref[...] / total_ref[0:1] + linear + bias_ref[...]
        out_ref[...] = (0.5 * pre * (1.0 + lax.erf(pre * math.sqrt(0.5)))).astype(out_ref.dtype)


def synthesize(place, et, xf, full, features, lin_weight, bias, total):
    rows = et.shape[0]
    modes = full.shape[0]
    width = full.shape[1] // 2
    whole = lambda j, place: (0, 0)
    return pl.pallas_call(
        synthesize_kernel,
        out_shape=jax.ShapeDtypeStruct((rows, width), jnp.bfloat16),
        grid_spec=pltpu.PrefetchScalarGridSpec(
            num_scalar_prefetch=1,
            grid=(HALF,),
            in_specs=[
                pl.BlockSpec((rows, 2 * PLANE), whole),
                pl.BlockSpec((1, rows, 2), lambda j, place: (j, 0, 0)),
                pl.BlockSpec((modes, 2 * width), whole),
                pl.BlockSpec((rows, width), whole),
                pl.BlockSpec((width, width), whole),
                pl.BlockSpec((1, width), whole),
                pl.BlockSpec((8, width), whole),
            ],
            out_specs=pl.BlockSpec((rows, width), whole),
            scratch_shapes=[
                pltpu.VMEM((modes, width), jnp.float32),
                pltpu.VMEM((modes, width), jnp.float32),
                pltpu.VMEM((4, PLANE, width), jnp.float32),
                pltpu.VMEM((rows, width), jnp.float32),
            ],
        ),
        compiler_params=pltpu.CompilerParams(vmem_limit_bytes=56 << 20),
    )(place, et, xf, full, features, lin_weight, bias[None, :], total)


def exchange_kernel(sizes, coef_ref, weight_ref, share_ref, out_ref, total_ref, w_ref, share_out, share_in, came0, came1, came2, came3, sum1, sum2, sum3, w_sem, sends, recvs, share_sends, share_recvs):
    n_x, n_y, n_z = sizes
    chunks, rows, wide = coef_ref.shape[1], coef_ref.shape[3], coef_ref.shape[4]
    width = wide // 2
    x, y, z = (lax.axis_index(a) for a in ("x", "modes", "z"))
    core = lax.axis_index("core")
    f32 = jnp.float32
    bf16 = jnp.bfloat16

    loads = []
    for k in range(chunks):
        part = pl.ds(k * rows, rows)
        loads.append(pltpu.make_async_copy(weight_ref.at[part], w_ref.at[part], w_sem.at[k]))
        loads[-1].start()

    peers = [{"core": 1 - core}]
    for axis, at, n in (("x", x, n_x), ("modes", y, n_y), ("z", z, n_z)):
        peers += [{axis: lax.rem(at + o, n)} for o in range(1, n)]
    barrier = pltpu.get_barrier_semaphore()
    for peer in peers:
        pl.semaphore_signal(barrier, inc=1, device_id=peer, device_id_type=pl.DeviceIdType.MESH)
    pl.semaphore_wait(barrier, len(peers))

    started = []

    def send(stage, k, o, src, dst, peer):
        copy = pltpu.make_async_remote_copy(
            src_ref=src,
            dst_ref=dst,
            send_sem=sends.at[stage, k, o - 1],
            recv_sem=recvs.at[stage, k, o - 1],
            device_id=peer,
            device_id_type=pl.DeviceIdType.MESH,
        )
        copy.start()
        started.append(copy)
        return copy

    def plan(k):
        if k % 2 == 0:
            return ("x", x, n_x), ("modes", y, n_y)
        return ("modes", y, n_y), ("x", x, n_x)

    def partial(k, base, count, level):
        (_, at1, n1), (_, at2, n2) = plan(k)
        total = coef_ref[core, k, pl.ds(base, count)].astype(f32) + came0[k, pl.ds(base, count)].astype(f32)
        if level >= 1:
            inner = base - at1 * (n2 * n_z)
            for o in range(n1 - 1):
                total += came1[k, pl.ds(o * n2 * n_z + inner, count)].astype(f32)
        if level >= 2:
            inner = inner - at2 * n_z
            for o in range(n2 - 1):
                total += came2[k, pl.ds(o * n_z + inner, count)].astype(f32)
        return total

    got = {}

    def scatter1(k):
        got[0, k][0].wait_recv()
        (axis, at, n), (_, _, n2) = plan(k)
        count = n2 * n_z
        copies = []
        for o in range(1, n):
            to = lax.rem(at + o, n)
            slot = pl.ds((o - 1) * count, count)
            sum1[k, slot] = partial(k, to * count, count, 0).astype(bf16)
            copies.append(send(1, k, o, sum1.at[k, slot], came1.at[k, slot], {axis: to}))
        got[1, k] = copies

    def scatter2(k):
        for copy in got[1, k]:
            copy.wait_recv()
        (_, at1, _), (axis, at, n) = plan(k)
        copies = []
        for o in range(1, n):
            to = lax.rem(at + o, n)
            slot = pl.ds((o - 1) * n_z, n_z)
            sum2[k, slot] = partial(k, (at1 * n + to) * n_z, n_z, 1).astype(bf16)
            copies.append(send(2, k, o, sum2.at[k, slot], came2.at[k, slot], {axis: to}))
        got[2, k] = copies

    def own_base(k):
        (_, at1, _), (_, at2, n2) = plan(k)
        return (at1 * n2 + at2) * n_z

    def scatter3(k):
        for copy in got[2, k]:
            copy.wait_recv()
        copies = []
        for o in range(1, n_z):
            to = lax.rem(z + o, n_z)
            slot = pl.ds(o - 1, 1)
            sum3[k, slot] = partial(k, own_base(k) + to, 1, 2).astype(bf16)
            copies.append(send(3, k, o, sum3.at[k, slot], came3.at[k, slot], {"z": to}))
        got[3, k] = copies

    def mix(k):
        for copy in got[3, k]:
            copy.wait_recv()
        total = partial(k, own_base(k) + z, 1, 2)[0]
        for o in range(n_z - 1):
            total += came3[k, o].astype(f32)
        coef = total.astype(bf16)
        re, im = coef[:, :width], coef[:, width:]
        lhs = jnp.concatenate(
            [jnp.concatenate([re, -im], axis=1), jnp.concatenate([im, re], axis=1)], axis=0
        )
        ids = lax.rem(lax.broadcasted_iota(jnp.int32, (2 * rows, width), 0), rows)
        loads[k].wait()
        unroll = 4

        def body(step, acc):
            for i in range(unroll):
                m = step * unroll + i
                w = w_ref[k * rows + m].reshape(2 * width, width)
                res = jnp.dot(lhs, w, preferred_element_type=f32)
                acc = jnp.where(ids == m, res, acc)
            return acc

        acc = lax.fori_loop(0, rows // unroll, body, jnp.zeros((2 * rows, width), f32))
        block = own_base(k) + z
        out_ref[core, k, block, :, :width] = acc[:rows].astype(bf16)
        out_ref[core, k, block, :, width:] = acc[rows:].astype(bf16)
        where = out_ref.at[core, k, block]
        got[4, k] = [send(4, k, o, where, where, {"z": lax.rem(z + o, n_z)}) for o in range(1, n_z)]

    def gather2(k):
        for copy in got[4, k]:
            copy.wait_recv()
        _, (axis, at, n) = plan(k)
        where = out_ref.at[core, k, pl.ds(own_base(k), n_z)]
        got[5, k] = [send(5, k, o, where, where, {axis: lax.rem(at + o, n)}) for o in range(1, n)]

    def gather1(k):
        for copy in got[5, k]:
            copy.wait_recv()
        (axis, at, n), (_, _, n2) = plan(k)
        count = n2 * n_z
        where = out_ref.at[core, k, pl.ds(at * count, count)]
        got[6, k] = [send(6, k, o, where, where, {axis: lax.rem(at + o, n)}) for o in range(1, n)]

    def gather0(k):
        for copy in got[6, k]:
            copy.wait_recv()
        where = out_ref.at[core, k]
        got[7, k] = [send(7, k, 1, where, where, {"core": 1 - core})]

    axes = (("core", core, 2), ("x", x, n_x), ("modes", y, n_y), ("z", z, n_z))
    shares = {}

    def share_step(level):
        axis, at, n = axes[level]
        share_out[level] = share_ref[...] if level == 0 else share_sum(level)
        shares[level] = []
        for o in range(1, n):
            copy = pltpu.make_async_remote_copy(
                src_ref=share_out.at[level],
                dst_ref=share_in.at[level, o - 1],
                send_sem=share_sends.at[level, o - 1],
                recv_sem=share_recvs.at[level, o - 1],
                device_id={axis: lax.rem(at + o, n)},
                device_id_type=pl.DeviceIdType.MESH,
            )
            copy.start()
            started.append(copy)
            shares[level].append(copy)

    def share_sum(level):
        value = share_out[level - 1]
        for o, copy in enumerate(shares[level - 1]):
            copy.wait_recv()
            value += share_in[level - 1, o]
        return value

    for k in range(chunks):
        got[0, k] = [send(0, k, 1, coef_ref.at[1 - core, k], came0.at[k], {"core": 1 - core})]
    stages = [scatter1, scatter2, scatter3, mix, gather2, gather1, gather0]
    lag = 2
    levels = len(axes)
    for t in range(chunks + lag * (len(stages) - 1)):
        for s in reversed(range(len(stages))):
            if 0 <= t - lag * s < chunks:
                stages[s](t - lag * s)
        if t % lag == 0 and t // lag < levels:
            share_step(t // lag)
        elif t == lag * levels:
            total_ref[...] = share_sum(levels)
    for k in range(chunks):
        got[7, k][0].wait_recv()
    for copy in started:
        copy.wait_send()


def exchange(coef, weight, share, sizes):
    n_x, n_y, n_z = sizes
    _, chunks, blocks, rows, wide = coef.shape
    width = wide // 2
    one = max((n_x - 1) * n_y, (n_y - 1) * n_x) * n_z
    two = max(n_x - 1, n_y - 1) * n_z
    three = max(n_z - 1, 1)
    hops = max(n_x, n_y, n_z, 2) - 1

    def buf(n):
        return pltpu.VMEM((chunks, n, rows, wide), jnp.bfloat16)

    return pl.pallas_call(
        functools.partial(exchange_kernel, sizes),
        out_shape=(jax.ShapeDtypeStruct(coef.shape, jnp.bfloat16), jax.ShapeDtypeStruct(share.shape, jnp.float32)),
        in_specs=[
            pl.BlockSpec(memory_space=pltpu.VMEM),
            pl.BlockSpec(memory_space=pl.ANY),
            pl.BlockSpec(memory_space=pltpu.VMEM),
        ],
        out_specs=(pl.BlockSpec(memory_space=pltpu.VMEM), pl.BlockSpec(memory_space=pltpu.VMEM)),
        scratch_shapes=[
            pltpu.VMEM(weight.shape, jnp.bfloat16),
            pltpu.VMEM((4,) + share.shape, jnp.float32),
            pltpu.VMEM((4, hops) + share.shape, jnp.float32),
            buf(blocks), buf(one), buf(two), buf(three), buf(one), buf(two), buf(three),
            pltpu.SemaphoreType.DMA((chunks,)),
            pltpu.SemaphoreType.DMA((8, chunks, hops)),
            pltpu.SemaphoreType.DMA((8, chunks, hops)),
            pltpu.SemaphoreType.DMA((4, hops)),
            pltpu.SemaphoreType.DMA((4, hops)),
        ],
        compiler_params=pltpu.CompilerParams(
            collective_id=0, has_side_effects=True, vmem_limit_bytes=48 << 20
        ),
    )(coef, weight, share)


def chunk_rows(own):
    chunks = max(2, min(8, own // 16))
    return chunks, own // chunks


def place_of(mode, sizes, own):
    n_x, n_y, n_z = sizes
    chunks, rows = chunk_rows(own)
    device, row = mode // own, mode % own
    y, pair = device % n_y, device // n_y
    core, chip = pair % 2, pair // 2
    x, z = chip % n_x, chip // n_x
    k = row // rows
    block = jnp.where(k % 2 == 0, x * n_y + y, y * n_x + x) * n_z + z
    return ((core * chunks + k) * (n_x * n_y * n_z) + block) * rows + row % rows


def grid_index(mode_table):
    kx = mode_table[0]
    slot = jnp.where(kx >= 0, kx, HALF - 1 - kx)
    return (slot * KY_COUNT + mode_table[1] - KY_LOW) * KZ_COUNT + mode_table[2] - KZ_LOW


def inverse_index(index):
    n = index.shape[0]
    lo = 128
    hi = n // lo
    ids = jnp.arange(n, dtype=jnp.int32)
    hot_lo = (index[:, None] % lo == jnp.arange(lo)[None, :]).astype(jnp.bfloat16)
    hit = index[None, :] // lo == jnp.arange(hi)[:, None]
    top = jnp.where(hit, ids[None, :] // lo, 0).astype(jnp.bfloat16)
    low = jnp.where(hit, ids[None, :] % lo, 0).astype(jnp.bfloat16)
    got = jnp.dot(jnp.concatenate([top, low], axis=0), hot_lo, preferred_element_type=jnp.float32)
    return (got[:hi] * lo + got[hi:]).astype(jnp.int32).reshape(n)


def on_device(features, coords, quad_weight, mode_table, mode_weight, lin_weight, bias):
    width = features.shape[1]
    sizes = tuple(lax.axis_size(a) for a in ("x", "modes", "z"))
    group = lax.axis_index("modes")
    rows = features.shape[0] // sizes[1]
    features = lax.dynamic_slice_in_dim(features, group * rows, rows, 0)
    coords = lax.dynamic_slice_in_dim(coords, group * rows, rows, 1)
    quad = lax.dynamic_slice_in_dim(quad_weight, group * rows, rows, 0)
    own = mode_weight.shape[0]
    xc, xs, parts = factors(coords)
    e, et = plane_factors(parts)
    inverse = inverse_index(grid_index(mode_table))
    place = place_of(inverse, sizes, own)
    weighted = (quad[:, None] * features.astype(jnp.float32)).astype(jnp.bfloat16).astype(jnp.float32)
    coef = analyse(place, e, jnp.concatenate([xc, xs], axis=0), weighted.T)
    chunks, step = chunk_rows(own)
    share = jnp.full((8, width), jnp.sum(quad), jnp.float32)
    full, total = exchange(coef.reshape(2, chunks, -1, step, 2 * width), mode_weight, share, sizes)
    xf = jnp.stack([xc, xs], axis=2)
    return synthesize(place, et, xf, full.reshape(-1, 2 * width), features, lin_weight, bias, total)


def solution(mesh):
    chips = mesh.shape["pts"] // 2
    n_x = 2 if chips % 2 == 0 else 1
    shape = (chips // n_x, n_x, 2, mesh.shape["modes"])
    mesh = Mesh(mesh.devices.reshape(shape), AXES)
    return jax.shard_map(
        on_device,
        mesh=mesh,
        in_specs=(
            P(PTS, None),
            P(None, PTS),
            P(PTS),
            P(),
            P(AXES, None, None, None),
            P(),
            P(),
        ),
        out_specs=P(AXES, None),
        check_vma=False,
    )
```

```python
import functools
import math

import jax
import jax.numpy as jnp
from jax import lax
from jax.experimental import pallas as pl
from jax.experimental.pallas import tpu as pltpu
from jax.sharding import Mesh
from jax.sharding import PartitionSpec as P

KX_LOW, KX_COUNT = -8, 16
KY_LOW, KY_COUNT = -8, 16
KZ_LOW, KZ_COUNT = 0, 32
HALF = KX_COUNT // 2
PLANE = KY_COUNT * KZ_COUNT
PTS = ("z", "x", "core")
AXES = PTS + ("modes",)


def cos_sin(turns):
    angle = (2.0 * math.pi) * (turns - jnp.round(turns))
    return jnp.cos(angle), jnp.sin(angle)


def factors(coords):
    x, y, z = coords[0], coords[1], coords[2]
    j = jnp.arange(HALF, dtype=jnp.float32) + 0.5
    xc, xs = cos_sin(j[:, None] * x[None, :])
    ky = jnp.arange(KY_COUNT, dtype=jnp.float32) + KY_LOW
    kz = jnp.arange(KZ_COUNT, dtype=jnp.float32) + KZ_LOW
    yc, ys = cos_sin(ky[:, None] * y[None, :])
    zc, zs = cos_sin(kz[:, None] * z[None, :] - 0.5 * x[None, :])
    return xc, xs, (yc, ys, zc, zs)


def plane_kernel(yc_ref, ys_ref, zc_ref, zs_ref, e_ref, et_ref):
    zc, zs = zc_ref[...], zs_ref[...]
    for k in range(KY_COUNT):
        yc, ys = yc_ref[pl.ds(k, 1)], ys_ref[pl.ds(k, 1)]
        re = yc * zc - ys * zs
        im = ys * zc + yc * zs
        e_ref[pl.ds(k * KZ_COUNT, KZ_COUNT)] = re.astype(jnp.bfloat16)
        e_ref[pl.ds(PLANE + k * KZ_COUNT, KZ_COUNT)] = im.astype(jnp.bfloat16)
    et_ref[...] = e_ref[...].T


def plane_factors(parts):
    rows = parts[0].shape[1]
    step = math.gcd(rows, 512)
    return pl.pallas_call(
        plane_kernel,
        grid=(rows // step,),
        out_shape=(
            jax.ShapeDtypeStruct((2 * PLANE, rows), jnp.bfloat16),
            jax.ShapeDtypeStruct((rows, 2 * PLANE), jnp.bfloat16),
        ),
        in_specs=[pl.BlockSpec((part.shape[0], step), lambda p: (0, p)) for part in parts],
        out_specs=(
            pl.BlockSpec((2 * PLANE, step), lambda p: (0, p)),
            pl.BlockSpec((step, 2 * PLANE), lambda p: (p, 0)),
        ),
        compiler_params=pltpu.CompilerParams(vmem_limit_bytes=48 << 20),
    )(*parts)


def analyse_kernel(e_ref, xt_ref, weighted_ref, re_tab, im_tab):
    j = pl.program_id(0)
    width = weighted_ref.shape[0]
    by_cos = (xt_ref[pl.ds(j, 1)] * weighted_ref[...]).astype(jnp.bfloat16)
    by_sin = (xt_ref[pl.ds(HALF + j, 1)] * weighted_ref[...]).astype(jnp.bfloat16)
    rhs = jnp.concatenate([by_cos, by_sin], axis=0)
    dims = (((1,), (1,)), ((), ()))
    re = lax.dot_general(e_ref[:PLANE], rhs, dims, preferred_element_type=jnp.float32)
    im = lax.dot_general(e_ref[PLANE:], rhs, dims, preferred_element_type=jnp.float32)
    rc, rs = re[:, :width], re[:, width:]
    ic, is_ = im[:, :width], im[:, width:]
    pos = pl.ds(pl.multiple_of(j * PLANE, PLANE), PLANE)
    neg = pl.ds(pl.multiple_of((HALF + j) * PLANE, PLANE), PLANE)
    re_tab[pos] = rc - is_
    im_tab[pos] = -(ic + rs)
    re_tab[neg] = rc + is_
    im_tab[neg] = rs - ic


def analyse(e, xt, weighted):
    width, rows = weighted.shape
    modes = 2 * HALF * PLANE
    whole = pl.BlockSpec(memory_space=pltpu.VMEM)
    table = jax.ShapeDtypeStruct((modes, width), jnp.float32)
    return pl.pallas_call(
        analyse_kernel,
        out_shape=(table, table),
        grid=(HALF,),
        in_specs=[whole, whole, whole],
        out_specs=(whole, whole),
        compiler_params=pltpu.CompilerParams(vmem_limit_bytes=24 << 20),
    )(e, xt, weighted)


def synthesize_kernel(
    place_ref, et_ref, xf_ref, full_ref, features_ref, lin_ref, bias_ref, total_ref, out_ref,
    re_tab, im_tab, stage, acc_ref, turn_ref, wave_ref,
):
    step = pl.program_id(0)
    last = pl.num_programs(0) - 1
    rows, width = out_ref.shape
    f32 = jnp.float32

    def move(q):
        slot = lax.rem(step, 2)
        for half in range(2):
            at = pl.ds(place_ref[(half * HALF + step) * PLANE + q], 1)
            stage[slot, 2 * half, pl.ds(q, 1)] = re_tab[at]
            stage[slot, 2 * half + 1, pl.ds(q, 1)] = im_tab[at]

    def fetch():
        unroll = 16

        @pl.loop(0, PLANE // unroll)
        def _(block):
            for i in range(unroll):
                move(block * unroll + i)

    def multiply():
        slot = lax.rem(step - 1, 2)
        pr, pi, nr, ni = (stage[slot, i] for i in range(4))
        top = jnp.concatenate([pr + nr, ni - pi], axis=1).astype(jnp.bfloat16)
        low = jnp.concatenate([-(pi + ni), nr - pr], axis=1).astype(jnp.bfloat16)
        field = jnp.dot(et_ref[:, :PLANE], top, preferred_element_type=f32)
        field = field + jnp.dot(et_ref[:, PLANE:], low, preferred_element_type=f32)
        xc, xs = wave_ref[slot, 0], wave_ref[slot, 1]
        acc_ref[...] += xc * field[:, :width] + xs * field[:, width:]
        turn = turn_ref[...]
        wave_ref[1 - slot, 0] = turn * xc - wave_ref[1 - slot, 0]
        wave_ref[1 - slot, 1] = turn * xs - wave_ref[1 - slot, 1]

    @pl.when(step == 0)
    def _():
        n = 256

        @pl.loop(0, full_ref.shape[0] // n)
        def _(i):
            at = pl.ds(pl.multiple_of(i * n, n), n)
            re_tab[at] = full_ref[at, :width].astype(f32)
            im_tab[at] = full_ref[at, width:].astype(f32)

        acc_ref[...] = jnp.zeros_like(acc_ref)
        shape = (rows, width)
        turn_ref[...] = jnp.broadcast_to(xf_ref[:, 0:1], shape)
        xc = jnp.broadcast_to(xf_ref[:, 1:2], shape)
        xs = jnp.broadcast_to(xf_ref[:, 2:3], shape)
        wave_ref[0, 0] = xc
        wave_ref[0, 1] = xs
        wave_ref[1, 0] = xc
        wave_ref[1, 1] = -xs

    @pl.when(step < last)
    def _():
        fetch()

    @pl.when(step > 0)
    def _():
        multiply()

    @pl.when(step == last)
    def _():
        linear = jnp.dot(features_ref[...], lin_ref[...], preferred_element_type=f32)
        pre = acc_ref[...] / total_ref[0:1] + linear + bias_ref[...]
        out_ref[...] = (0.5 * pre * (1.0 + lax.erf(pre * math.sqrt(0.5)))).astype(out_ref.dtype)


def synthesize(place, et, xf, full, features, lin_weight, bias, total):
    rows = et.shape[0]
    modes = full.shape[0]
    width = full.shape[1] // 2
    whole = pl.BlockSpec(memory_space=pltpu.VMEM)
    return pl.pallas_call(
        synthesize_kernel,
        out_shape=jax.ShapeDtypeStruct((rows, width), jnp.bfloat16),
        grid_spec=pltpu.PrefetchScalarGridSpec(
            num_scalar_prefetch=1,
            grid=(HALF + 1,),
            in_specs=[whole] * 7,
            out_specs=pl.BlockSpec((rows, width), lambda j, place: (0, 0)),
            scratch_shapes=[
                pltpu.VMEM((modes, width), jnp.float32),
                pltpu.VMEM((modes, width), jnp.float32),
                pltpu.VMEM((2, 4, PLANE, width), jnp.float32),
                pltpu.VMEM((rows, width), jnp.float32),
                pltpu.VMEM((rows, width), jnp.float32),
                pltpu.VMEM((2, 2, rows, width), jnp.float32),
            ],
        ),
        compiler_params=pltpu.CompilerParams(vmem_limit_bytes=28 << 20),
    )(place, et, xf, full, features, lin_weight, bias[None, :], total)


def exchange_kernel(
    sizes, order_ref, re_tab, im_tab, weight_ref, share_ref, out_ref, total_ref, coef_ref, pick, w_ref, share_out, share_in,
    came0, came1, came2, came3, sum1, sum2, sum3, w_sem, sends, recvs, share_sends, share_recvs,
):
    n_x, n_y, n_z = sizes
    _, chunks, blocks, rows, wide = coef_ref.shape
    width = wide // 2
    x, y, z = (lax.axis_index(a) for a in ("x", "modes", "z"))
    core = lax.axis_index("core")
    f32 = jnp.float32
    bf16 = jnp.bfloat16

    loads = []
    for k in range(chunks):
        part = pl.ds(k * rows, rows)
        loads.append(pltpu.make_async_copy(weight_ref.at[part], w_ref.at[part], w_sem.at[k]))
        loads[-1].start()

    peers = [{"core": 1 - core}]
    for axis, at, n in (("x", x, n_x), ("modes", y, n_y), ("z", z, n_z)):
        peers += [{axis: lax.rem(at + o, n)} for o in range(1, n)]
    barrier = pltpu.get_barrier_semaphore()
    for peer in peers:
        pl.semaphore_signal(barrier, inc=1, device_id=peer, device_id_type=pl.DeviceIdType.MESH)
    pl.semaphore_wait(barrier, len(peers))

    started = []

    def send(stage, k, o, src, dst, peer):
        copy = pltpu.make_async_remote_copy(
            src_ref=src,
            dst_ref=dst,
            send_sem=sends.at[stage, k, o - 1],
            recv_sem=recvs.at[stage, k, o - 1],
            device_id=peer,
            device_id_type=pl.DeviceIdType.MESH,
        )
        copy.start()
        started.append(copy)
        return copy

    def plan(k):
        if k % 2 == 0:
            return ("x", x, n_x), ("modes", y, n_y)
        return ("modes", y, n_y), ("x", x, n_x)

    def partial(k, base, count, level):
        (_, at1, n1), (_, at2, n2) = plan(k)
        total = coef_ref[core, k, pl.ds(base, count)].astype(f32) + came0[k, pl.ds(base, count)].astype(f32)
        if level >= 1:
            inner = base - at1 * (n2 * n_z)
            for o in range(n1 - 1):
                total += came1[k, pl.ds(o * n2 * n_z + inner, count)].astype(f32)
        if level >= 2:
            inner = inner - at2 * n_z
            for o in range(n2 - 1):
                total += came2[k, pl.ds(o * n_z + inner, count)].astype(f32)
        return total

    got = {}

    def fetch(side, k):
        count = blocks * rows
        base = (side * chunks + k) * count
        unroll = 16

        def body(block, carry):
            for i in range(unroll):
                q = block * unroll + i
                at = pl.ds(order_ref[base + q], 1)
                pick[0, pl.ds(q, 1)] = re_tab[at]
                pick[1, pl.ds(q, 1)] = im_tab[at]
            return carry

        lax.fori_loop(0, count // unroll, body, 0)
        for half in range(2):
            part = pick[half].astype(bf16).reshape(blocks, rows, width)
            coef_ref[side, k, :, :, half * width : (half + 1) * width] = part

    def scatter0(k):
        fetch(1 - core, k)
        got[0, k] = [send(0, k, 1, coef_ref.at[1 - core, k], came0.at[k], {"core": 1 - core})]
        fetch(core, k)

    def scatter1(k):
        got[0, k][0].wait_recv()
        (axis, at, n), (_, _, n2) = plan(k)
        count = n2 * n_z
        copies = []
        for o in range(1, n):
            to = lax.rem(at + o, n)
            slot = pl.ds((o - 1) * count, count)
            sum1[k, slot] = partial(k, to * count, count, 0).astype(bf16)
            copies.append(send(1, k, o, sum1.at[k, slot], came1.at[k, slot], {axis: to}))
        got[1, k] = copies

    def scatter2(k):
        for copy in got[1, k]:
            copy.wait_recv()
        (_, at1, _), (axis, at, n) = plan(k)
        copies = []
        for o in range(1, n):
            to = lax.rem(at + o, n)
            slot = pl.ds((o - 1) * n_z, n_z)
            sum2[k, slot] = partial(k, (at1 * n + to) * n_z, n_z, 1).astype(bf16)
            copies.append(send(2, k, o, sum2.at[k, slot], came2.at[k, slot], {axis: to}))
        got[2, k] = copies

    def own_base(k):
        (_, at1, _), (_, at2, n2) = plan(k)
        return (at1 * n2 + at2) * n_z

    def scatter3(k):
        for copy in got[2, k]:
            copy.wait_recv()
        copies = []
        for o in range(1, n_z):
            to = lax.rem(z + o, n_z)
            slot = pl.ds(o - 1, 1)
            sum3[k, slot] = partial(k, own_base(k) + to, 1, 2).astype(bf16)
            copies.append(send(3, k, o, sum3.at[k, slot], came3.at[k, slot], {"z": to}))
        got[3, k] = copies

    def mix(k):
        for copy in got[3, k]:
            copy.wait_recv()
        total = partial(k, own_base(k) + z, 1, 2)[0]
        for o in range(n_z - 1):
            total += came3[k, o].astype(f32)
        coef = total.astype(bf16)
        re, im = coef[:, :width], coef[:, width:]
        lhs = jnp.concatenate(
            [jnp.concatenate([re, -im], axis=1), jnp.concatenate([im, re], axis=1)], axis=0
        )
        ids = lax.rem(lax.broadcasted_iota(jnp.int32, (2 * rows, width), 0), rows)
        loads[k].wait()
        unroll = 4

        def body(step, acc):
            for i in range(unroll):
                m = step * unroll + i
                w = w_ref[k * rows + m].reshape(2 * width, width)
                res = jnp.dot(lhs, w, preferred_element_type=f32)
                acc = jnp.where(ids == m, res, acc)
            return acc

        acc = lax.fori_loop(0, rows // unroll, body, jnp.zeros((2 * rows, width), f32))
        block = own_base(k) + z
        out_ref[core, k, block, :, :width] = acc[:rows].astype(bf16)
        out_ref[core, k, block, :, width:] = acc[rows:].astype(bf16)
        where = out_ref.at[core, k, block]
        got[4, k] = [send(4, k, o, where, where, {"z": lax.rem(z + o, n_z)}) for o in range(1, n_z)]

    def gather2(k):
        for copy in got[4, k]:
            copy.wait_recv()
        _, (axis, at, n) = plan(k)
        where = out_ref.at[core, k, pl.ds(own_base(k), n_z)]
        got[5, k] = [send(5, k, o, where, where, {axis: lax.rem(at + o, n)}) for o in range(1, n)]

    def gather1(k):
        for copy in got[5, k]:
            copy.wait_recv()
        (axis, at, n), (_, _, n2) = plan(k)
        count = n2 * n_z
        where = out_ref.at[core, k, pl.ds(at * count, count)]
        got[6, k] = [send(6, k, o, where, where, {axis: lax.rem(at + o, n)}) for o in range(1, n)]

    def gather0(k):
        for copy in got[6, k]:
            copy.wait_recv()
        where = out_ref.at[core, k]
        got[7, k] = [send(7, k, 1, where, where, {"core": 1 - core})]

    axes = (("core", core, 2), ("x", x, n_x), ("modes", y, n_y), ("z", z, n_z))
    shares = {}

    def share_step(level):
        axis, at, n = axes[level]
        share_out[level] = share_ref[...] if level == 0 else share_sum(level)
        shares[level] = []
        for o in range(1, n):
            copy = pltpu.make_async_remote_copy(
                src_ref=share_out.at[level],
                dst_ref=share_in.at[level, o - 1],
                send_sem=share_sends.at[level, o - 1],
                recv_sem=share_recvs.at[level, o - 1],
                device_id={axis: lax.rem(at + o, n)},
                device_id_type=pl.DeviceIdType.MESH,
            )
            copy.start()
            started.append(copy)
            shares[level].append(copy)

    def share_sum(level):
        value = share_out[level - 1]
        for o, copy in enumerate(shares[level - 1]):
            copy.wait_recv()
            value += share_in[level - 1, o]
        return value

    stages = [scatter0, scatter1, scatter2, scatter3, mix, gather2, gather1, gather0]
    lag = 2
    levels = len(axes)
    starts = [0] + [1 + lag * s for s in range(len(stages) - 1)]
    for t in range(chunks + starts[-1]):
        for s in reversed(range(len(stages))):
            if 0 <= t - starts[s] < chunks:
                stages[s](t - starts[s])
        if t % lag == 0 and t // lag < levels:
            share_step(t // lag)
        elif t == lag * levels:
            total_ref[...] = share_sum(levels)
    for k in range(chunks):
        got[7, k][0].wait_recv()
    for copy in started:
        copy.wait_send()


def exchange(order, re_tab, im_tab, weight, share, sizes):
    n_x, n_y, n_z = sizes
    chunks, rows = chunk_rows(weight.shape[0])
    blocks = n_x * n_y * n_z
    width = weight.shape[-1]
    wide = 2 * width
    shape = (2, chunks, blocks, rows, wide)
    one = max((n_x - 1) * n_y, (n_y - 1) * n_x) * n_z
    two = max(n_x - 1, n_y - 1) * n_z
    three = max(n_z - 1, 1)
    hops = max(n_x, n_y, n_z, 2) - 1

    def buf(n):
        return pltpu.VMEM((chunks, n, rows, wide), jnp.bfloat16)

    return pl.pallas_call(
        functools.partial(exchange_kernel, sizes),
        out_shape=(jax.ShapeDtypeStruct(shape, jnp.bfloat16), jax.ShapeDtypeStruct(share.shape, jnp.float32)),
        in_specs=[
            pl.BlockSpec(memory_space=pltpu.SMEM),
            pl.BlockSpec(memory_space=pltpu.VMEM),
            pl.BlockSpec(memory_space=pltpu.VMEM),
            pl.BlockSpec(memory_space=pl.ANY),
            pl.BlockSpec(memory_space=pltpu.VMEM),
        ],
        out_specs=(pl.BlockSpec(memory_space=pltpu.VMEM), pl.BlockSpec(memory_space=pltpu.VMEM)),
        scratch_shapes=[
            pltpu.VMEM(shape, jnp.bfloat16),
            pltpu.VMEM((2, blocks * rows, width), jnp.float32),
            pltpu.VMEM(weight.shape, jnp.bfloat16),
            pltpu.VMEM((4,) + share.shape, jnp.float32),
            pltpu.VMEM((4, hops) + share.shape, jnp.float32),
            buf(blocks), buf(one), buf(two), buf(three), buf(one), buf(two), buf(three),
            pltpu.SemaphoreType.DMA((chunks,)),
            pltpu.SemaphoreType.DMA((8, chunks, hops)),
            pltpu.SemaphoreType.DMA((8, chunks, hops)),
            pltpu.SemaphoreType.DMA((4, hops)),
            pltpu.SemaphoreType.DMA((4, hops)),
        ],
        compiler_params=pltpu.CompilerParams(
            collective_id=0, has_side_effects=True, vmem_limit_bytes=36 << 20
        ),
    )(order, re_tab, im_tab, weight, share)


def chunk_rows(own):
    chunks = max(2, min(8, own // 16))
    return chunks, own // chunks


def to_layout(values, sizes, own):
    n_x, n_y, n_z = sizes
    chunks, rows = chunk_rows(own)
    v = values.reshape(n_z, n_x, 2, n_y, chunks // 2, 2, rows)
    even = v[:, :, :, :, :, 0].transpose(2, 4, 1, 3, 0, 5).reshape(2, chunks // 2, -1)
    odd = v[:, :, :, :, :, 1].transpose(2, 4, 3, 1, 0, 5).reshape(2, chunks // 2, -1)
    return jnp.stack([even, odd], axis=2).reshape(-1)


def place_of(mode, sizes, own):
    n_x, n_y, n_z = sizes
    chunks, rows = chunk_rows(own)
    device, row = mode // own, mode % own
    y, pair = device % n_y, device // n_y
    core, chip = pair % 2, pair // 2
    x, z = chip % n_x, chip // n_x
    k = row // rows
    block = jnp.where(k % 2 == 0, x * n_y + y, y * n_x + x) * n_z + z
    return ((core * chunks + k) * (n_x * n_y * n_z) + block) * rows + row % rows


def grid_index(mode_table):
    kx = mode_table[0]
    slot = jnp.where(kx >= 0, kx, HALF - 1 - kx)
    return (slot * KY_COUNT + mode_table[1] - KY_LOW) * KZ_COUNT + mode_table[2] - KZ_LOW


def inverse_index(index):
    n = index.shape[0]
    lo = 128
    hi = n // lo
    ids = jnp.arange(n, dtype=jnp.int32)
    hot_lo = (index[:, None] % lo == jnp.arange(lo)[None, :]).astype(jnp.bfloat16)
    hit = index[None, :] // lo == jnp.arange(hi)[:, None]
    top = jnp.where(hit, ids[None, :] // lo, 0).astype(jnp.bfloat16)
    low = jnp.where(hit, ids[None, :] % lo, 0).astype(jnp.bfloat16)
    got = jnp.dot(jnp.concatenate([top, low], axis=0), hot_lo, preferred_element_type=jnp.float32)
    return (got[:hi] * lo + got[hi:]).astype(jnp.int32).reshape(n)


def on_device(features, coords, quad_weight, mode_table, mode_weight, lin_weight, bias):
    width = features.shape[1]
    sizes = tuple(lax.axis_size(a) for a in ("x", "modes", "z"))
    group = lax.axis_index("modes")
    rows = features.shape[0] // sizes[1]
    features = lax.dynamic_slice_in_dim(features, group * rows, rows, 0)
    coords = lax.dynamic_slice_in_dim(coords, group * rows, rows, 1)
    quad = lax.dynamic_slice_in_dim(quad_weight, group * rows, rows, 0)
    own = mode_weight.shape[0]
    xc, xs, parts = factors(coords)
    e, et = plane_factors(parts)
    index = grid_index(mode_table)
    order = to_layout(index, sizes, own)
    place = place_of(inverse_index(index), sizes, own)
    weighted = (quad[:, None] * features.astype(jnp.float32)).astype(jnp.bfloat16).astype(jnp.float32)
    re_tab, im_tab = analyse(e, jnp.concatenate([xc, xs], axis=0), weighted.T)
    share = jnp.full((8, width), jnp.sum(quad), jnp.float32)
    full, total = exchange(order, re_tab, im_tab, mode_weight, share, sizes)
    turn = 2.0 * cos_sin(coords[0])[0]
    xf = jnp.pad(jnp.stack([turn, xc[0], xs[0]], axis=1), ((0, 0), (0, width - 3)))
    return synthesize(place, et, xf, full.reshape(-1, 2 * width), features, lin_weight, bias, total)


def solution(mesh):
    chips = mesh.shape["pts"] // 2
    n_x = 2 if chips % 2 == 0 else 1
    shape = (chips // n_x, n_x, 2, mesh.shape["modes"])
    mesh = Mesh(mesh.devices.reshape(shape), AXES)
    return jax.shard_map(
        on_device,
        mesh=mesh,
        in_specs=(
            P(PTS, None),
            P(None, PTS),
            P(PTS),
            P(),
            P(AXES, None, None, None),
            P(),
            P(),
        ),
        out_specs=P(AXES, None),
        check_vma=False,
    )
```

```python
import functools
import math

import jax
import jax.numpy as jnp
from jax import lax
from jax.experimental import pallas as pl
from jax.experimental.pallas import tpu as pltpu
from jax.sharding import Mesh
from jax.sharding import PartitionSpec as P

KX_LOW, KX_COUNT = -8, 16
KY_LOW, KY_COUNT = -8, 16
KZ_LOW, KZ_COUNT = 0, 32
HALF = KX_COUNT // 2
PLANE = KY_COUNT * KZ_COUNT
PTS = ("z", "x", "core")
AXES = PTS + ("modes",)
PAD = 8


def product(a, b):
    return a[0] * b[0] - a[1] * b[1], a[0] * b[1] + a[1] * b[0]


def powers(out_c, out_s, start, unit, count):
    out_c[0:1], out_s[0:1] = start
    n = 1
    while n < count:
        out_c[n : 2 * n], out_s[n : 2 * n] = product((out_c[0:n], out_s[0:n]), unit)
        unit = product(unit, unit)
        n *= 2
    return unit


def analyse_kernel(coords_ref, quad_ref, features_ref, *refs):
    e_ref, tab, xt_ref, share_ref, weighted, yc, ys, zc, zs = refs[-9:]
    j = pl.program_id(0)
    width = weighted.shape[0]
    bf16 = jnp.bfloat16

    @pl.when(j == 0)
    def _():
        base = coords_ref[...]
        turns = jnp.concatenate([0.5 * base[0:1], base[1:3]], axis=0)
        angle = (2.0 * math.pi) * (turns - jnp.round(turns))
        cos, sin = jnp.cos(angle), jnp.sin(angle)
        half, y, z = ((cos[i : i + 1], sin[i : i + 1]) for i in range(3))
        powers(xt_ref.at[:HALF], xt_ref.at[HALF:], half, product(half, half), HALF)
        one = jnp.ones_like(half[0])
        mid = KY_COUNT // 2
        far = powers(yc.at[mid:], ys.at[mid:], (one, 0.0 * one), y, mid)
        far = (far[0], -far[1])
        yc[:mid], ys[:mid] = product((yc[mid:], ys[mid:]), far)
        powers(zc, zs, (half[0], -half[1]), z, KZ_COUNT)
        for k in range(KY_COUNT):
            re, im = product((yc[k : k + 1], ys[k : k + 1]), (zc[...], zs[...]))
            e_ref[pl.ds(k * KZ_COUNT, KZ_COUNT)] = re.astype(bf16)
            e_ref[pl.ds(PLANE + k * KZ_COUNT, KZ_COUNT)] = im.astype(bf16)
        quad = quad_ref[...]
        share_ref[...] = jnp.broadcast_to(jnp.sum(quad, axis=1, keepdims=True), share_ref.shape)
        scaled = quad * features_ref[...].astype(jnp.float32).T
        weighted[...] = scaled.astype(bf16).astype(jnp.float32)

    by_cos = (xt_ref[pl.ds(j, 1)] * weighted[...]).astype(bf16)
    by_sin = (xt_ref[pl.ds(HALF + j, 1)] * weighted[...]).astype(bf16)
    rhs = jnp.concatenate([by_cos, by_sin], axis=0)
    dims = (((1,), (1,)), ((), ()))
    re = lax.dot_general(e_ref[:PLANE], rhs, dims, preferred_element_type=jnp.float32)
    im = lax.dot_general(e_ref[PLANE:], rhs, dims, preferred_element_type=jnp.float32)
    rc, rs = re[:, :width], re[:, width:]
    ic, is_ = im[:, :width], im[:, width:]
    pos = pl.multiple_of(2 * j * PLANE, 2 * PLANE)
    neg = pl.multiple_of(2 * (HALF + j) * PLANE, 2 * PLANE)
    tab[pl.ds(pos, PLANE, stride=2)] = rc - is_
    tab[pl.ds(pos + 1, PLANE, stride=2)] = -(ic + rs)
    tab[pl.ds(neg, PLANE, stride=2)] = rc + is_
    tab[pl.ds(neg + 1, PLANE, stride=2)] = rs - ic


def analyse(coords, quad, features, *after):
    rows, width = features.shape
    f32 = jnp.float32
    whole = pl.BlockSpec(memory_space=pltpu.VMEM)
    return pl.pallas_call(
        analyse_kernel,
        out_shape=(
            jax.ShapeDtypeStruct((2 * PLANE, rows), jnp.bfloat16),
            jax.ShapeDtypeStruct((4 * HALF * PLANE + PAD, width), f32),
            jax.ShapeDtypeStruct((2 * HALF, rows), f32),
            jax.ShapeDtypeStruct((8, width), f32),
        ),
        grid=(HALF,),
        in_specs=[whole, whole, whole] + [pl.BlockSpec(memory_space=pl.ANY)] * len(after),
        out_specs=(whole,) * 4,
        scratch_shapes=[pltpu.VMEM((width, rows), f32)]
        + [pltpu.VMEM((n, rows), f32) for n in (KY_COUNT, KY_COUNT, KZ_COUNT, KZ_COUNT)],
        compiler_params=pltpu.CompilerParams(vmem_limit_bytes=16 << 20),
    )(coords, quad, features, *after)


def synthesize_kernel(
    order_ref, e_ref, xt_ref, full_ref, features_ref, lin_ref, bias_ref, total_ref, out_ref, tab, acc
):
    j = pl.program_id(0)
    width = out_ref.shape[1]
    f32 = jnp.float32

    @pl.when(j == 0)
    def _():
        unroll = 32

        @pl.loop(0, full_ref.shape[0] // (2 * unroll))
        def _(block):
            for i in range(unroll):
                q = block * unroll + i
                tab[pl.ds(pl.multiple_of(order_ref[q], 2), 2)] = full_ref[pl.ds(pl.multiple_of(2 * q, 2), 2)]

        acc[...] = jnp.zeros_like(acc)

    pos = pl.multiple_of(2 * j * PLANE, 2 * PLANE)
    neg = pl.multiple_of(2 * (HALF + j) * PLANE, 2 * PLANE)
    pr, pi, nr, ni = (tab[pl.ds(at, PLANE, stride=2)] for at in (pos, pos + 1, neg, neg + 1))
    top = jnp.concatenate([pr + nr, ni - pi], axis=1).astype(jnp.bfloat16)
    low = jnp.concatenate([-(pi + ni), nr - pr], axis=1).astype(jnp.bfloat16)
    rhs = jnp.concatenate([top, low], axis=0)
    dims = (((0,), (0,)), ((), ()))
    field = lax.dot_general(rhs, e_ref[...], dims, preferred_element_type=f32)
    acc[...] += xt_ref[pl.ds(j, 1)] * field[:width] + xt_ref[pl.ds(HALF + j, 1)] * field[width:]

    @pl.when(j == pl.num_programs(0) - 1)
    def _():
        linear = jnp.dot(features_ref[...], lin_ref[...], preferred_element_type=f32)
        pre = acc[...].T * (1.0 / total_ref[0:1]) + linear + bias_ref[...]
        out_ref[...] = (0.5 * pre * (1.0 + lax.erf(pre * math.sqrt(0.5)))).astype(out_ref.dtype)


def synthesize(order, e, xt, full, features, lin_weight, bias, total):
    rows, width = features.shape
    whole = pl.BlockSpec(memory_space=pltpu.VMEM)
    return pl.pallas_call(
        synthesize_kernel,
        out_shape=jax.ShapeDtypeStruct((rows, width), jnp.bfloat16),
        grid_spec=pltpu.PrefetchScalarGridSpec(
            num_scalar_prefetch=1,
            grid=(HALF,),
            in_specs=[whole] * 7,
            out_specs=pl.BlockSpec((rows, width), lambda j, order: (0, 0)),
            scratch_shapes=[pltpu.VMEM(full.shape, jnp.float32), pltpu.VMEM((width, rows), jnp.float32)],
        ),
        compiler_params=pltpu.CompilerParams(vmem_limit_bytes=16 << 20),
    )(order, e, xt, full, features, lin_weight, bias[None, :], total)


def exchange_kernel(
    sizes, order_ref, tab, weight_ref, share_ref, full_ref, total_ref, out_ref, coef_ref, pick, w_ref, share_out, share_in,
    came0, came1, came2, came3, sum1, sum2, sum3, w_sem, sends, recvs, share_sends, share_recvs,
):
    n_x, n_y, n_z = sizes
    _, chunks, blocks, rows, wide = coef_ref.shape
    width = wide // 2
    x, y, z = (lax.axis_index(a) for a in ("x", "modes", "z"))
    core = lax.axis_index("core")
    f32 = jnp.float32
    bf16 = jnp.bfloat16

    loads = []
    for k in range(chunks):
        part = pl.ds(k * rows, rows)
        loads.append(pltpu.make_async_copy(weight_ref.at[part], w_ref.at[part], w_sem.at[k]))
        loads[-1].start()

    peers = [{"core": 1 - core}]
    for axis, at, n in (("x", x, n_x), ("modes", y, n_y), ("z", z, n_z)):
        peers += [{axis: lax.rem(at + o, n)} for o in range(1, n)]
    barrier = pltpu.get_barrier_semaphore()
    for peer in peers:
        pl.semaphore_signal(barrier, inc=1, device_id=peer, device_id_type=pl.DeviceIdType.MESH)
    pl.semaphore_wait(barrier, len(peers))

    started = []

    def send(stage, k, o, src, dst, peer):
        copy = pltpu.make_async_remote_copy(
            src_ref=src,
            dst_ref=dst,
            send_sem=sends.at[stage, k, o - 1],
            recv_sem=recvs.at[stage, k, o - 1],
            device_id=peer,
            device_id_type=pl.DeviceIdType.MESH,
        )
        copy.start()
        started.append(copy)
        return copy

    def plan(k):
        if k % 2 == 0:
            return ("x", x, n_x), ("modes", y, n_y)
        return ("modes", y, n_y), ("x", x, n_x)

    def partial(k, base, count, level):
        (_, at1, n1), (_, at2, n2) = plan(k)
        total = coef_ref[core, k, pl.ds(base, count)].astype(f32) + came0[k, pl.ds(base, count)].astype(f32)
        if level >= 1:
            inner = base - at1 * (n2 * n_z)
            for o in range(n1 - 1):
                total += came1[k, pl.ds(o * n2 * n_z + inner, count)].astype(f32)
        if level >= 2:
            inner = inner - at2 * n_z
            for o in range(n2 - 1):
                total += came2[k, pl.ds(o * n_z + inner, count)].astype(f32)
        return total

    got = {}

    def fetch(side, k):
        count = blocks * rows
        base = (side * chunks + k) * count
        unroll = 16

        def body(block, carry):
            for i in range(unroll):
                q = block * unroll + i
                pick[pl.ds(pl.multiple_of(2 * q, 2), 2)] = tab[pl.ds(order_ref[base + q], 2)]
            return carry

        lax.fori_loop(0, count // unroll, body, 0)
        for half in range(2):
            part = pick[pl.ds(half, count, stride=2)].astype(bf16).reshape(blocks, rows, width)
            coef_ref[side, k, :, :, half * width : (half + 1) * width] = part

    def expand(k):
        got[7, k][0].wait_recv()
        count = blocks * rows
        for side in range(2):
            start = 2 * (side * chunks + k) * count
            for half in range(2):
                part = out_ref[side, k, :, :, half * width : (half + 1) * width]
                full_ref[pl.ds(start + half, count, stride=2)] = part.reshape(count, width).astype(f32)

    def scatter0(k):
        fetch(1 - core, k)
        got[0, k] = [send(0, k, 1, coef_ref.at[1 - core, k], came0.at[k], {"core": 1 - core})]
        fetch(core, k)

    def scatter1(k):
        got[0, k][0].wait_recv()
        (axis, at, n), (_, _, n2) = plan(k)
        count = n2 * n_z
        copies = []
        for o in range(1, n):
            to = lax.rem(at + o, n)
            slot = pl.ds((o - 1) * count, count)
            sum1[k, slot] = partial(k, to * count, count, 0).astype(bf16)
            copies.append(send(1, k, o, sum1.at[k, slot], came1.at[k, slot], {axis: to}))
        got[1, k] = copies

    def scatter2(k):
        for copy in got[1, k]:
            copy.wait_recv()
        (_, at1, _), (axis, at, n) = plan(k)
        copies = []
        for o in range(1, n):
            to = lax.rem(at + o, n)
            slot = pl.ds((o - 1) * n_z, n_z)
            sum2[k, slot] = partial(k, (at1 * n + to) * n_z, n_z, 1).astype(bf16)
            copies.append(send(2, k, o, sum2.at[k, slot], came2.at[k, slot], {axis: to}))
        got[2, k] = copies

    def own_base(k):
        (_, at1, _), (_, at2, n2) = plan(k)
        return (at1 * n2 + at2) * n_z

    def scatter3(k):
        for copy in got[2, k]:
            copy.wait_recv()
        copies = []
        for o in range(1, n_z):
            to = lax.rem(z + o, n_z)
            slot = pl.ds(o - 1, 1)
            sum3[k, slot] = partial(k, own_base(k) + to, 1, 2).astype(bf16)
            copies.append(send(3, k, o, sum3.at[k, slot], came3.at[k, slot], {"z": to}))
        got[3, k] = copies

    def mix(k):
        for copy in got[3, k]:
            copy.wait_recv()
        total = partial(k, own_base(k) + z, 1, 2)[0]
        for o in range(n_z - 1):
            total += came3[k, o].astype(f32)
        coef = total.astype(bf16)
        re, im = coef[:, :width], coef[:, width:]
        lhs = jnp.concatenate(
            [jnp.concatenate([re, -im], axis=1), jnp.concatenate([im, re], axis=1)], axis=0
        )
        ids = lax.rem(lax.broadcasted_iota(jnp.int32, (2 * rows, width), 0), rows)
        loads[k].wait()
        unroll = math.gcd(rows, 16)

        def body(step, acc):
            for i in range(unroll):
                m = step * unroll + i
                w = w_ref[k * rows + m].reshape(2 * width, width)
                res = jnp.dot(lhs, w, preferred_element_type=f32)
                acc = jnp.where(ids == m, res, acc)
            return acc

        acc = lax.fori_loop(0, rows // unroll, body, jnp.zeros((2 * rows, width), f32))
        block = own_base(k) + z
        out_ref[core, k, block, :, :width] = acc[:rows].astype(bf16)
        out_ref[core, k, block, :, width:] = acc[rows:].astype(bf16)
        where = out_ref.at[core, k, block]
        got[4, k] = [send(4, k, o, where, where, {"z": lax.rem(z + o, n_z)}) for o in range(1, n_z)]

    def gather2(k):
        for copy in got[4, k]:
            copy.wait_recv()
        _, (axis, at, n) = plan(k)
        where = out_ref.at[core, k, pl.ds(own_base(k), n_z)]
        got[5, k] = [send(5, k, o, where, where, {axis: lax.rem(at + o, n)}) for o in range(1, n)]

    def gather1(k):
        for copy in got[5, k]:
            copy.wait_recv()
        (axis, at, n), (_, _, n2) = plan(k)
        count = n2 * n_z
        where = out_ref.at[core, k, pl.ds(at * count, count)]
        got[6, k] = [send(6, k, o, where, where, {axis: lax.rem(at + o, n)}) for o in range(1, n)]

    def gather0(k):
        for copy in got[6, k]:
            copy.wait_recv()
        where = out_ref.at[core, k]
        got[7, k] = [send(7, k, 1, where, where, {"core": 1 - core})]

    axes = (("core", core, 2), ("x", x, n_x), ("modes", y, n_y), ("z", z, n_z))
    shares = {}

    def share_step(level):
        axis, at, n = axes[level]
        share_out[level] = share_ref[...] if level == 0 else share_sum(level)
        shares[level] = []
        for o in range(1, n):
            copy = pltpu.make_async_remote_copy(
                src_ref=share_out.at[level],
                dst_ref=share_in.at[level, o - 1],
                send_sem=share_sends.at[level, o - 1],
                recv_sem=share_recvs.at[level, o - 1],
                device_id={axis: lax.rem(at + o, n)},
                device_id_type=pl.DeviceIdType.MESH,
            )
            copy.start()
            started.append(copy)
            shares[level].append(copy)

    def share_sum(level):
        value = share_out[level - 1]
        for o, copy in enumerate(shares[level - 1]):
            copy.wait_recv()
            value += share_in[level - 1, o]
        return value

    stages = [scatter0, scatter1, scatter2, scatter3, mix, gather2, gather1, gather0, expand]
    lag = 2
    levels = len(axes)
    starts = [0] + [1 + lag * s for s in range(len(stages) - 1)]
    for t in range(chunks + starts[-1]):
        for s in reversed(range(len(stages))):
            if 0 <= t - starts[s] < chunks:
                stages[s](t - starts[s])
        if t % lag == 0 and t // lag < levels:
            share_step(t // lag)
        elif t == lag * levels:
            total_ref[...] = share_sum(levels)
    for copy in started:
        copy.wait_send()


def exchange(order, tab, weight, share, sizes):
    n_x, n_y, n_z = sizes
    chunks, rows = chunk_rows(weight.shape[0])
    blocks = n_x * n_y * n_z
    width = weight.shape[-1]
    wide = 2 * width
    shape = (2, chunks, blocks, rows, wide)
    one = max((n_x - 1) * n_y, (n_y - 1) * n_x) * n_z
    two = max(n_x - 1, n_y - 1) * n_z
    three = max(n_z - 1, 1)
    hops = max(n_x, n_y, n_z, 2) - 1

    def buf(n):
        return pltpu.VMEM((chunks, n, rows, wide), jnp.bfloat16)

    return pl.pallas_call(
        functools.partial(exchange_kernel, sizes),
        out_shape=(jax.ShapeDtypeStruct(tab.shape, jnp.float32), jax.ShapeDtypeStruct(share.shape, jnp.float32)),
        in_specs=[
            pl.BlockSpec(memory_space=pltpu.SMEM),
            pl.BlockSpec(memory_space=pltpu.VMEM),
            pl.BlockSpec(memory_space=pl.ANY),
            pl.BlockSpec(memory_space=pltpu.VMEM),
        ],
        out_specs=(pl.BlockSpec(memory_space=pltpu.VMEM), pl.BlockSpec(memory_space=pltpu.VMEM)),
        scratch_shapes=[
            pltpu.VMEM(shape, jnp.bfloat16),
            pltpu.VMEM(shape, jnp.bfloat16),
            pltpu.VMEM((2 * blocks * rows + PAD, width), jnp.float32),
            pltpu.VMEM(weight.shape, jnp.bfloat16),
            pltpu.VMEM((4,) + share.shape, jnp.float32),
            pltpu.VMEM((4, hops) + share.shape, jnp.float32),
            buf(blocks), buf(one), buf(two), buf(three), buf(one), buf(two), buf(three),
            pltpu.SemaphoreType.DMA((chunks,)),
            pltpu.SemaphoreType.DMA((8, chunks, hops)),
            pltpu.SemaphoreType.DMA((8, chunks, hops)),
            pltpu.SemaphoreType.DMA((4, hops)),
            pltpu.SemaphoreType.DMA((4, hops)),
        ],
        compiler_params=pltpu.CompilerParams(
            collective_id=0, has_side_effects=True, vmem_limit_bytes=36 << 20
        ),
    )(order, tab, weight, share)


def chunk_rows(own):
    chunks = max(2, min(8, own // 16))
    return chunks, own // chunks


def to_layout(values, sizes, own):
    n_x, n_y, n_z = sizes
    chunks, rows = chunk_rows(own)
    v = values.reshape(n_z, n_x, 2, n_y, chunks // 2, 2, rows)
    even = v[:, :, :, :, :, 0].transpose(2, 4, 1, 3, 0, 5).reshape(2, chunks // 2, -1)
    odd = v[:, :, :, :, :, 1].transpose(2, 4, 3, 1, 0, 5).reshape(2, chunks // 2, -1)
    return jnp.stack([even, odd], axis=2).reshape(-1)


def grid_index(mode_table):
    kx = mode_table[0]
    slot = jnp.where(kx >= 0, kx, HALF - 1 - kx)
    return (slot * KY_COUNT + mode_table[1] - KY_LOW) * KZ_COUNT + mode_table[2] - KZ_LOW


def on_device(features, coords, quad_weight, mode_table, mode_weight, lin_weight, bias):
    width = features.shape[1]
    sizes = tuple(lax.axis_size(a) for a in ("x", "modes", "z"))
    group = lax.axis_index("modes")
    rows = features.shape[0] // sizes[1]
    features = lax.dynamic_slice_in_dim(features, group * rows, rows, 0)
    coords = lax.dynamic_slice_in_dim(coords, group * rows, rows, 1)
    quad = lax.dynamic_slice_in_dim(quad_weight, group * rows, rows, 0)
    own = mode_weight.shape[0]
    order = 2 * to_layout(grid_index(mode_table), sizes, own)
    e, tab, xt, share = analyse(coords, quad[None, :], features, order)
    full, total = exchange(order, tab, mode_weight, share, sizes)
    return synthesize(order, e, xt, full, features, lin_weight, bias, total)


def solution(mesh):
    chips = mesh.shape["pts"] // 2
    n_x = 2 if chips % 2 == 0 else 1
    shape = (chips // n_x, n_x, 2, mesh.shape["modes"])
    mesh = Mesh(mesh.devices.reshape(shape), AXES)
    return jax.shard_map(
        on_device,
        mesh=mesh,
        in_specs=(
            P(PTS, None),
            P(None, PTS),
            P(PTS),
            P(),
            P(AXES, None, None, None),
            P(),
            P(),
        ),
        out_specs=P(AXES, None),
        check_vma=False,
    )
```

```python
import functools
import math

import jax
import jax.numpy as jnp
from jax import lax
from jax.experimental import pallas as pl
from jax.experimental.pallas import tpu as pltpu
from jax.sharding import Mesh
from jax.sharding import PartitionSpec as P

KX_LOW, KX_COUNT = -8, 16
KY_LOW, KY_COUNT = -8, 16
KZ_LOW, KZ_COUNT = 0, 32
HALF = KX_COUNT // 2
PLANE = KY_COUNT * KZ_COUNT
PTS = ("z", "x", "core")
AXES = PTS + ("modes",)
PAD = 8


def product(a, b):
    return a[0] * b[0] - a[1] * b[1], a[0] * b[1] + a[1] * b[0]


def powers(out_c, out_s, start, unit, count):
    out_c[0:1], out_s[0:1] = start
    n = 1
    while n < count:
        out_c[n : 2 * n], out_s[n : 2 * n] = product((out_c[0:n], out_s[0:n]), unit)
        unit = product(unit, unit)
        n *= 2
    return unit


def analyse_kernel(group_ref, coords_ref, quad_ref, features_ref, *refs):
    e_ref, tab, xt_ref, share_ref, weighted, yc, ys, zc, zs = refs[-9:]
    j = pl.program_id(0)
    width = weighted.shape[0]
    bf16 = jnp.bfloat16

    @pl.when(j == 0)
    def _():
        base = coords_ref[...]
        turns = jnp.concatenate([0.5 * base[0:1], base[1:3]], axis=0)
        angle = (2.0 * math.pi) * (turns - jnp.round(turns))
        cos, sin = jnp.cos(angle), jnp.sin(angle)
        half, y, z = ((cos[i : i + 1], sin[i : i + 1]) for i in range(3))
        powers(xt_ref.at[:HALF], xt_ref.at[HALF:], half, product(half, half), HALF)
        one = jnp.ones_like(half[0])
        mid = KY_COUNT // 2
        far = powers(yc.at[mid:], ys.at[mid:], (one, 0.0 * one), y, mid)
        far = (far[0], -far[1])
        yc[:mid], ys[:mid] = product((yc[mid:], ys[mid:]), far)
        powers(zc, zs, (half[0], -half[1]), z, KZ_COUNT)
        for k in range(KY_COUNT):
            re, im = product((yc[k : k + 1], ys[k : k + 1]), (zc[...], zs[...]))
            e_ref[pl.ds(k * KZ_COUNT, KZ_COUNT)] = re.astype(bf16)
            e_ref[pl.ds(PLANE + k * KZ_COUNT, KZ_COUNT)] = im.astype(bf16)
        quad = quad_ref[...]
        share_ref[...] = jnp.broadcast_to(jnp.sum(quad, axis=1, keepdims=True), share_ref.shape)
        scaled = quad * features_ref[...].astype(jnp.float32).T
        weighted[...] = scaled.astype(bf16).astype(jnp.float32)

    by_cos = (xt_ref[pl.ds(j, 1)] * weighted[...]).astype(bf16)
    by_sin = (xt_ref[pl.ds(HALF + j, 1)] * weighted[...]).astype(bf16)
    rhs = jnp.concatenate([by_cos, by_sin], axis=0)
    dims = (((1,), (1,)), ((), ()))
    re = lax.dot_general(e_ref[:PLANE], rhs, dims, preferred_element_type=jnp.float32)
    im = lax.dot_general(e_ref[PLANE:], rhs, dims, preferred_element_type=jnp.float32)
    rc, rs = re[:, :width], re[:, width:]
    ic, is_ = im[:, :width], im[:, width:]
    pos = pl.multiple_of(2 * j * PLANE, 2 * PLANE)
    neg = pl.multiple_of(2 * (HALF + j) * PLANE, 2 * PLANE)
    tab[pl.ds(pos, PLANE, stride=2)] = rc - is_
    tab[pl.ds(pos + 1, PLANE, stride=2)] = -(ic + rs)
    tab[pl.ds(neg, PLANE, stride=2)] = rc + is_
    tab[pl.ds(neg + 1, PLANE, stride=2)] = rs - ic


def analyse(group, rows, coords, quad, features, *after):
    width = features.shape[1]
    f32 = jnp.float32
    whole = pl.BlockSpec(memory_space=pltpu.VMEM)
    return pl.pallas_call(
        analyse_kernel,
        out_shape=(
            jax.ShapeDtypeStruct((2 * PLANE, rows), jnp.bfloat16),
            jax.ShapeDtypeStruct((4 * HALF * PLANE + PAD, width), f32),
            jax.ShapeDtypeStruct((2 * HALF, rows), f32),
            jax.ShapeDtypeStruct((8, width), f32),
        ),
        grid_spec=pltpu.PrefetchScalarGridSpec(
            num_scalar_prefetch=1,
            grid=(HALF,),
            in_specs=[
                pl.BlockSpec((3, rows), lambda j, group: (0, group[0])),
                pl.BlockSpec((1, rows), lambda j, group: (0, group[0])),
                pl.BlockSpec((rows, width), lambda j, group: (group[0], 0)),
            ]
            + [pl.BlockSpec(memory_space=pl.ANY)] * len(after),
            out_specs=(whole,) * 4,
            scratch_shapes=[pltpu.VMEM((width, rows), f32)]
            + [pltpu.VMEM((n, rows), f32) for n in (KY_COUNT, KY_COUNT, KZ_COUNT, KZ_COUNT)],
        ),
        compiler_params=pltpu.CompilerParams(vmem_limit_bytes=16 << 20),
    )(group, coords, quad, features, *after)


def synthesize_kernel(
    order_ref, group_ref, e_ref, xt_ref, full_ref, features_ref, lin_ref, bias_ref, total_ref, out_ref, tab, acc
):
    j = pl.program_id(0)
    width = out_ref.shape[1]
    f32 = jnp.float32

    @pl.when(j == 0)
    def _():
        unroll = 32

        @pl.loop(0, full_ref.shape[0] // (2 * unroll))
        def _(block):
            for i in range(unroll):
                q = block * unroll + i
                tab[pl.ds(pl.multiple_of(order_ref[q], 2), 2)] = full_ref[pl.ds(pl.multiple_of(2 * q, 2), 2)]

        acc[...] = jnp.zeros_like(acc)

    pos = pl.multiple_of(2 * j * PLANE, 2 * PLANE)
    neg = pl.multiple_of(2 * (HALF + j) * PLANE, 2 * PLANE)
    pr, pi, nr, ni = (tab[pl.ds(at, PLANE, stride=2)] for at in (pos, pos + 1, neg, neg + 1))
    top = jnp.concatenate([pr + nr, ni - pi], axis=1).astype(jnp.bfloat16)
    low = jnp.concatenate([-(pi + ni), nr - pr], axis=1).astype(jnp.bfloat16)
    rhs = jnp.concatenate([top, low], axis=0)
    dims = (((0,), (0,)), ((), ()))
    field = lax.dot_general(rhs, e_ref[...], dims, preferred_element_type=f32)
    acc[...] += xt_ref[pl.ds(j, 1)] * field[:width] + xt_ref[pl.ds(HALF + j, 1)] * field[width:]

    @pl.when(j == pl.num_programs(0) - 1)
    def _():
        linear = jnp.dot(features_ref[...], lin_ref[...], preferred_element_type=f32)
        pre = acc[...].T * (1.0 / total_ref[0:1]) + linear + bias_ref[...]
        out_ref[...] = (0.5 * pre * (1.0 + lax.erf(pre * math.sqrt(0.5)))).astype(out_ref.dtype)


def synthesize(order, group, e, xt, full, features, lin_weight, bias, total):
    rows, width = e.shape[1], features.shape[1]
    whole = pl.BlockSpec(memory_space=pltpu.VMEM)
    return pl.pallas_call(
        synthesize_kernel,
        out_shape=jax.ShapeDtypeStruct((rows, width), jnp.bfloat16),
        grid_spec=pltpu.PrefetchScalarGridSpec(
            num_scalar_prefetch=2,
            grid=(HALF,),
            in_specs=[whole] * 3
            + [pl.BlockSpec((rows, width), lambda j, order, group: (group[0], 0))]
            + [whole] * 3,
            out_specs=pl.BlockSpec((rows, width), lambda j, order, group: (0, 0)),
            scratch_shapes=[pltpu.VMEM(full.shape, jnp.float32), pltpu.VMEM((width, rows), jnp.float32)],
        ),
        compiler_params=pltpu.CompilerParams(vmem_limit_bytes=16 << 20),
    )(order, group, e, xt, full, features, lin_weight, bias[None, :], total)


def chunk_plan(own):
    axes = ("x", "modes", "z"), ("modes", "x", "z")
    chunks = max(2, min(8, own // 16))
    return [(own // chunks, axes[k % 2]) for k in range(chunks)]


class Geometry:
    def __init__(self, own, sizes):
        self.sizes = sizes
        self.plan = chunk_plan(own)
        self.blocks = math.prod(sizes.values())
        self.modes = self.blocks * own
        self.first, self.start = [], []
        self.held = [0] * 4
        done = 0
        for rows, axes in self.plan:
            self.first.append(done)
            done += rows
            self.start.append(list(self.held))
            self.held[0] += self.blocks * rows
            for s in (1, 2, 3):
                self.held[s] += (sizes[axes[s - 1]] - 1) * self.stride(axes, s) * rows

    def stride(self, axes, s):
        return math.prod(self.sizes[a] for a in axes[s:])


def span(start, size):
    return pl.ds(pl.multiple_of(start, 16), size)


def exchange_kernel(own, sizes, index_ref, tab, weight_ref, share_ref, full_ref, total_ref, *scratch):
    out_ref, coef_ref, pick, w_ref, share_out, share_in = scratch[:6]
    came, sums = scratch[6:10], (None,) + scratch[10:13]
    w_sem, sends, recvs, share_sends, share_recvs = scratch[13:]
    geo = Geometry(own, sizes)
    width = full_ref.shape[1]
    at = {a: lax.axis_index(a) for a in sizes}
    core = lax.axis_index("core")
    f32 = jnp.float32
    bf16 = jnp.bfloat16
    plan = geo.plan
    chunks = len(plan)

    loads = []
    for k, (rows, _) in enumerate(plan):
        part = pl.ds(geo.first[k], rows)
        loads.append(pltpu.make_async_copy(weight_ref.at[part], w_ref.at[part], w_sem.at[k]))
        loads[-1].start()

    def peer(axis, o):
        return {axis: lax.rem(at[axis] + o, sizes[axis])}

    peers = [{"core": 1 - core}]
    for axis, n in sizes.items():
        peers += [peer(axis, o) for o in range(1, n)]
    barrier = pltpu.get_barrier_semaphore()
    for p in peers:
        pl.semaphore_signal(barrier, inc=1, device_id=p, device_id_type=pl.DeviceIdType.MESH)
    pl.semaphore_wait(barrier, len(peers))

    started = []
    got = {}

    def send(stage, k, o, src, dst, to):
        copy = pltpu.make_async_remote_copy(
            src_ref=src,
            dst_ref=dst,
            send_sem=sends.at[stage, k, o - 1],
            recv_sem=recvs.at[stage, k, o - 1],
            device_id=to,
            device_id_type=pl.DeviceIdType.MESH,
        )
        copy.start()
        started.append(copy)
        return copy

    def arrive(stage, k):
        for copy in got[stage, k]:
            copy.wait_recv()

    def base_of(k, levels):
        axes = plan[k][1]
        return sum((at[axes[s - 1]] * geo.stride(axes, s) for s in range(1, levels + 1)), 0)

    def device_row(k, block, side):
        axes = plan[k][1]
        pos = {a: block // geo.stride(axes, s + 1) % sizes[a] for s, a in enumerate(axes)}
        chip = pos["z"] * sizes["x"] + pos["x"]
        return ((chip * 2 + side) * sizes["modes"] + pos["modes"]) * own + geo.first[k]

    def home(side, k, block):
        return side * geo.modes + geo.start[k][0] + block * plan[k][0]

    def partial(k, base, count, level):
        rows, axes = plan[k]
        total = coef_ref[span(home(core, k, base), count * rows)].astype(f32)
        total += came[0][span(home(0, k, base), count * rows)].astype(f32)
        inner = base
        for s in range(1, level + 1):
            stride = geo.stride(axes, s)
            inner = inner - at[axes[s - 1]] * stride
            for o in range(sizes[axes[s - 1]] - 1):
                lo = geo.start[k][s] + (o * stride + inner) * rows
                total += came[s][span(lo, count * rows)].astype(f32)
        return total

    def fetch(side, k):
        rows = plan[k][0]

        def body(block, carry):
            base = device_row(k, block, side)
            for i in range(rows):
                pick[pl.ds(2 * (block * rows + i), 2)] = tab[pl.ds(index_ref[base + i], 2)]
            return carry

        lax.fori_loop(0, geo.blocks, body, 0)
        count = geo.blocks * rows
        for half in range(2):
            part = pick[pl.ds(half, count, stride=2)].astype(bf16)
            coef_ref[span(home(side, k, 0), count), half * width : (half + 1) * width] = part

    def scatter0(k):
        fetch(1 - core, k)
        count = geo.blocks * plan[k][0]
        src = coef_ref.at[span(home(1 - core, k, 0), count)]
        got[0, k] = [send(0, k, 1, src, came[0].at[span(home(0, k, 0), count)], {"core": 1 - core})]
        fetch(core, k)

    def scatter(s):
        def run(k):
            arrive(s - 1, k)
            rows, axes = plan[k]
            axis, stride = axes[s - 1], geo.stride(axes, s)
            got[s, k] = []
            for o in range(1, sizes[axis]):
                to = peer(axis, o)
                slot = span(geo.start[k][s] + (o - 1) * stride * rows, stride * rows)
                sums[s][slot] = partial(k, base_of(k, s - 1) + to[axis] * stride, stride, s - 1).astype(bf16)
                got[s, k].append(send(s, k, o, sums[s].at[slot], came[s].at[slot], to))

        return run

    def mix(k):
        arrive(3, k)
        rows = plan[k][0]
        coef = partial(k, base_of(k, 3), 1, 3).astype(bf16)
        re, im = coef[:, :width], coef[:, width:]
        lhs = jnp.concatenate(
            [jnp.concatenate([re, -im], axis=1), jnp.concatenate([im, re], axis=1)], axis=0
        )
        ids = lax.rem(lax.broadcasted_iota(jnp.int32, (2 * rows, width), 0), rows)
        loads[k].wait()
        unroll = 16

        def body(step, acc):
            for i in range(unroll):
                m = step * unroll + i
                w = w_ref[geo.first[k] + m].reshape(2 * width, width)
                res = jnp.dot(lhs, w, preferred_element_type=f32)
                acc = jnp.where(ids == m, res, acc)
            return acc

        acc = lax.fori_loop(0, rows // unroll, body, jnp.zeros((2 * rows, width), f32))
        where = span(home(core, k, base_of(k, 3)), rows)
        out_ref[where, :width] = acc[:rows].astype(bf16)
        out_ref[where, width:] = acc[rows:].astype(bf16)

    def gather(s):
        def run(k):
            if s == 3:
                mix(k)
            else:
                arrive(7 - s - 1, k)
            rows, axes = plan[k]
            axis, stride = axes[s - 1], geo.stride(axes, s)
            where = out_ref.at[span(home(core, k, base_of(k, s)), stride * rows)]
            got[7 - s, k] = [send(7 - s, k, o, where, where, peer(axis, o)) for o in range(1, sizes[axis])]

        return run

    def gather0(k):
        arrive(6, k)
        where = out_ref.at[span(home(core, k, 0), geo.blocks * plan[k][0])]
        got[7, k] = [send(7, k, 1, where, where, {"core": 1 - core})]

    def expand(k):
        arrive(7, k)
        rows = plan[k][0]

        def body(block, carry):
            for side in range(2):
                to = 2 * device_row(k, block, side)
                values = out_ref[span(home(side, k, block), rows)].astype(f32)
                for half in range(2):
                    full_ref[pl.ds(to + half, rows, stride=2)] = values[:, half * width : (half + 1) * width]
            return carry

        lax.fori_loop(0, geo.blocks, body, 0)

    axes = (("core", 2),) + tuple(sizes.items())
    shares = {}

    def share_sum(level):
        value = share_out[level - 1]
        for o, copy in enumerate(shares[level - 1]):
            copy.wait_recv()
            value += share_in[level - 1, o]
        return value

    def share_step(level):
        axis, n = axes[level]
        share_out[level] = share_ref[...] if level == 0 else share_sum(level)
        shares[level] = []
        for o in range(1, n):
            copy = pltpu.make_async_remote_copy(
                src_ref=share_out.at[level],
                dst_ref=share_in.at[level, o - 1],
                send_sem=share_sends.at[level, o - 1],
                recv_sem=share_recvs.at[level, o - 1],
                device_id={"core": 1 - core} if level == 0 else peer(axis, o),
                device_id_type=pl.DeviceIdType.MESH,
            )
            copy.start()
            started.append(copy)
            shares[level].append(copy)

    stages = [scatter0, scatter(1), scatter(2), scatter(3), gather(3), gather(2), gather(1), gather0, expand]
    starts = [0] + [1 + 2 * s for s in range(len(stages) - 1)]
    for t in range(chunks + starts[-1]):
        for s in reversed(range(len(stages))):
            if 0 <= t - starts[s] < chunks:
                stages[s](t - starts[s])
        if t % 2 == 0 and t // 2 < len(axes):
            share_step(t // 2)
        elif t == 2 * len(axes):
            total_ref[...] = share_sum(len(axes))
    for copy in started:
        copy.wait_send()


def exchange(index, tab, weight, share, sizes):
    own, width = weight.shape[0], weight.shape[-1]
    geo = Geometry(own, sizes)
    chunks = len(geo.plan)
    hops = max(2, *sizes.values()) - 1
    held = [max(n, 16) for n in geo.held]

    def buf(n):
        return pltpu.VMEM((n, 2 * width), jnp.bfloat16)

    vmem = pl.BlockSpec(memory_space=pltpu.VMEM)
    return pl.pallas_call(
        functools.partial(exchange_kernel, own, sizes),
        out_shape=(jax.ShapeDtypeStruct(tab.shape, jnp.float32), jax.ShapeDtypeStruct(share.shape, jnp.float32)),
        in_specs=[pl.BlockSpec(memory_space=pltpu.SMEM), vmem, pl.BlockSpec(memory_space=pl.ANY), vmem],
        out_specs=(vmem, vmem),
        scratch_shapes=[
            buf(2 * geo.modes),
            buf(2 * geo.modes),
            pltpu.VMEM((2 * geo.blocks * max(rows for rows, _ in geo.plan) + PAD, width), jnp.float32),
            pltpu.VMEM(weight.shape, jnp.bfloat16),
            pltpu.VMEM((4,) + share.shape, jnp.float32),
            pltpu.VMEM((4, hops) + share.shape, jnp.float32),
            buf(held[0]), buf(held[1]), buf(held[2]), buf(held[3]),
            buf(held[1]), buf(held[2]), buf(held[3]),
            pltpu.SemaphoreType.DMA((chunks,)),
            pltpu.SemaphoreType.DMA((8, chunks, hops)),
            pltpu.SemaphoreType.DMA((8, chunks, hops)),
            pltpu.SemaphoreType.DMA((4, hops)),
            pltpu.SemaphoreType.DMA((4, hops)),
        ],
        compiler_params=pltpu.CompilerParams(
            collective_id=0, has_side_effects=True, vmem_limit_bytes=35 << 20
        ),
    )(index, tab, weight, share)


def grid_index(mode_table):
    kx = mode_table[0]
    slot = jnp.where(kx >= 0, kx, HALF - 1 - kx)
    return (slot * KY_COUNT + mode_table[1] - KY_LOW) * KZ_COUNT + mode_table[2] - KZ_LOW


def on_device(features, coords, quad_weight, mode_table, mode_weight, lin_weight, bias):
    sizes = {a: lax.axis_size(a) for a in ("x", "modes", "z")}
    rows = features.shape[0] // sizes["modes"]
    group = lax.axis_index("modes")[None]
    index = 2 * grid_index(mode_table)
    e, tab, xt, share = analyse(group, rows, coords, quad_weight[None, :], features, index)
    full, total = exchange(index, tab, mode_weight, share, sizes)
    return synthesize(index, group, e, xt, full, features, lin_weight, bias, total)


def solution(mesh):
    chips = mesh.shape["pts"] // 2
    n_x = 2 if chips % 2 == 0 else 1
    shape = (chips // n_x, n_x, 2, mesh.shape["modes"])
    mesh = Mesh(mesh.devices.reshape(shape), AXES)
    return jax.shard_map(
        on_device,
        mesh=mesh,
        in_specs=(
            P(PTS, None),
            P(None, PTS),
            P(PTS),
            P(),
            P(AXES, None, None, None),
            P(),
            P(),
        ),
        out_specs=P(AXES, None),
        check_vma=False,
    )
```

```python
import functools
import math

import jax
import jax.numpy as jnp
from jax import lax
from jax.experimental import pallas as pl
from jax.experimental.pallas import tpu as pltpu
from jax.sharding import Mesh
from jax.sharding import PartitionSpec as P

KX_LOW, KX_COUNT = -8, 16
KY_LOW, KY_COUNT = -8, 16
KZ_LOW, KZ_COUNT = 0, 32
HALF = KX_COUNT // 2
PLANE = KY_COUNT * KZ_COUNT
PTS = ("z", "x", "core")
AXES = PTS + ("modes",)
PAD = 8


def product(a, b):
    return a[0] * b[0] - a[1] * b[1], a[0] * b[1] + a[1] * b[0]


def powers(out_c, out_s, start, unit, count):
    out_c[0:1], out_s[0:1] = start
    n = 1
    while n < count:
        out_c[n : 2 * n], out_s[n : 2 * n] = product((out_c[0:n], out_s[0:n]), unit)
        unit = product(unit, unit)
        n *= 2
    return unit


def analyse_kernel(group_ref, coords_ref, quad_ref, features_ref, *refs):
    e_ref, tab, xt_ref, share_ref, weighted, yc, ys, zc, zs = refs[-9:]
    j = pl.program_id(0)
    width = weighted.shape[0]
    bf16 = jnp.bfloat16

    @pl.when(j == 0)
    def _():
        base = coords_ref[...]
        turns = jnp.concatenate([0.5 * base[0:1], base[1:3]], axis=0)
        angle = (2.0 * math.pi) * (turns - jnp.round(turns))
        cos, sin = jnp.cos(angle), jnp.sin(angle)
        half, y, z = ((cos[i : i + 1], sin[i : i + 1]) for i in range(3))
        powers(xt_ref.at[:HALF], xt_ref.at[HALF:], half, product(half, half), HALF)
        one = jnp.ones_like(half[0])
        mid = KY_COUNT // 2
        far = powers(yc.at[mid:], ys.at[mid:], (one, 0.0 * one), y, mid)
        far = (far[0], -far[1])
        yc[:mid], ys[:mid] = product((yc[mid:], ys[mid:]), far)
        powers(zc, zs, (half[0], -half[1]), z, KZ_COUNT)
        for k in range(KY_COUNT):
            re, im = product((yc[k : k + 1], ys[k : k + 1]), (zc[...], zs[...]))
            e_ref[pl.ds(k * KZ_COUNT, KZ_COUNT)] = re.astype(bf16)
            e_ref[pl.ds(PLANE + k * KZ_COUNT, KZ_COUNT)] = im.astype(bf16)
        quad = quad_ref[...]
        share_ref[...] = jnp.broadcast_to(jnp.sum(quad, axis=1, keepdims=True), share_ref.shape)
        scaled = quad * features_ref[...].astype(jnp.float32).T
        weighted[...] = scaled.astype(bf16).astype(jnp.float32)

    by_cos = (xt_ref[pl.ds(j, 1)] * weighted[...]).astype(bf16)
    by_sin = (xt_ref[pl.ds(HALF + j, 1)] * weighted[...]).astype(bf16)
    rhs = jnp.concatenate([by_cos, by_sin], axis=0)
    dims = (((1,), (1,)), ((), ()))
    re = lax.dot_general(e_ref[:PLANE], rhs, dims, preferred_element_type=jnp.float32)
    im = lax.dot_general(e_ref[PLANE:], rhs, dims, preferred_element_type=jnp.float32)
    rc, rs = re[:, :width], re[:, width:]
    ic, is_ = im[:, :width], im[:, width:]
    pos = pl.multiple_of(2 * j * PLANE, 2 * PLANE)
    neg = pl.multiple_of(2 * (HALF + j) * PLANE, 2 * PLANE)
    tab[pl.ds(pos, PLANE, stride=2)] = rc - is_
    tab[pl.ds(pos + 1, PLANE, stride=2)] = -(ic + rs)
    tab[pl.ds(neg, PLANE, stride=2)] = rc + is_
    tab[pl.ds(neg + 1, PLANE, stride=2)] = rs - ic


def analyse(group, rows, coords, quad, features, *after):
    width = features.shape[1]
    f32 = jnp.float32
    whole = pl.BlockSpec(memory_space=pltpu.VMEM)
    return pl.pallas_call(
        analyse_kernel,
        out_shape=(
            jax.ShapeDtypeStruct((2 * PLANE, rows), jnp.bfloat16),
            jax.ShapeDtypeStruct((4 * HALF * PLANE + PAD, width), f32),
            jax.ShapeDtypeStruct((2 * HALF, rows), f32),
            jax.ShapeDtypeStruct((8, width), f32),
        ),
        grid_spec=pltpu.PrefetchScalarGridSpec(
            num_scalar_prefetch=1,
            grid=(HALF,),
            in_specs=[
                pl.BlockSpec((3, rows), lambda j, group: (0, group[0])),
                pl.BlockSpec((1, rows), lambda j, group: (0, group[0])),
                pl.BlockSpec((rows, width), lambda j, group: (group[0], 0)),
            ]
            + [pl.BlockSpec(memory_space=pl.ANY)] * len(after),
            out_specs=(whole,) * 4,
            scratch_shapes=[pltpu.VMEM((width, rows), f32)]
            + [pltpu.VMEM((n, rows), f32) for n in (KY_COUNT, KY_COUNT, KZ_COUNT, KZ_COUNT)],
        ),
        compiler_params=pltpu.CompilerParams(vmem_limit_bytes=16 << 20),
    )(group, coords, quad, features, *after)


def synthesize_kernel(
    order_ref, group_ref, e_ref, xt_ref, full_ref, features_ref, lin_ref, bias_ref, total_ref, out_ref, tab, acc
):
    j = pl.program_id(0)
    width = out_ref.shape[1]
    f32 = jnp.float32

    @pl.when(j == 0)
    def _():
        unroll = math.gcd(full_ref.shape[0] // 2 - PAD // 2, 128)

        @pl.loop(0, full_ref.shape[0] // (2 * unroll))
        def _(block):
            for i in range(unroll):
                q = block * unroll + i
                tab[pl.ds(pl.multiple_of(order_ref[q], 2), 2)] = full_ref[pl.ds(pl.multiple_of(2 * q, 2), 2)]

        acc[...] = jnp.zeros_like(acc)

    pos = pl.multiple_of(2 * j * PLANE, 2 * PLANE)
    neg = pl.multiple_of(2 * (HALF + j) * PLANE, 2 * PLANE)
    pr, pi, nr, ni = (tab[pl.ds(at, PLANE, stride=2)] for at in (pos, pos + 1, neg, neg + 1))
    top = jnp.concatenate([pr + nr, ni - pi], axis=1).astype(jnp.bfloat16)
    low = jnp.concatenate([-(pi + ni), nr - pr], axis=1).astype(jnp.bfloat16)
    rhs = jnp.concatenate([top, low], axis=0)
    dims = (((0,), (0,)), ((), ()))
    field = lax.dot_general(rhs, e_ref[...], dims, preferred_element_type=f32)
    acc[...] += xt_ref[pl.ds(j, 1)] * field[:width] + xt_ref[pl.ds(HALF + j, 1)] * field[width:]

    @pl.when(j == pl.num_programs(0) - 1)
    def _():
        linear = jnp.dot(features_ref[...], lin_ref[...], preferred_element_type=f32)
        pre = acc[...].T * (1.0 / total_ref[0:1]) + linear + bias_ref[...]
        out_ref[...] = (0.5 * pre * (1.0 + lax.erf(pre * math.sqrt(0.5)))).astype(out_ref.dtype)


def synthesize(order, group, e, xt, full, features, lin_weight, bias, total):
    rows, width = e.shape[1], features.shape[1]
    whole = pl.BlockSpec(memory_space=pltpu.VMEM)
    return pl.pallas_call(
        synthesize_kernel,
        out_shape=jax.ShapeDtypeStruct((rows, width), jnp.bfloat16),
        grid_spec=pltpu.PrefetchScalarGridSpec(
            num_scalar_prefetch=2,
            grid=(HALF,),
            in_specs=[whole] * 3
            + [pl.BlockSpec((rows, width), lambda j, order, group: (group[0], 0))]
            + [whole] * 3,
            out_specs=pl.BlockSpec((rows, width), lambda j, order, group: (0, 0)),
            scratch_shapes=[pltpu.VMEM(full.shape, jnp.float32), pltpu.VMEM((width, rows), jnp.float32)],
        ),
        compiler_params=pltpu.CompilerParams(vmem_limit_bytes=16 << 20),
    )(order, group, e, xt, full, features, lin_weight, bias[None, :], total)


def chunk_plan(own):
    axes = ("x", "modes", "z"), ("modes", "x", "z")
    chunks = max(2, min(8, own // 16))
    return [(own // chunks, axes[k % 2]) for k in range(chunks)]


class Geometry:
    def __init__(self, own, sizes):
        self.sizes = sizes
        self.plan = chunk_plan(own)
        self.blocks = math.prod(sizes.values())
        self.modes = self.blocks * own
        self.first, self.start = [], []
        self.held = [0] * 4
        done = 0
        for rows, axes in self.plan:
            self.first.append(done)
            done += rows
            self.start.append(list(self.held))
            self.held[0] += self.blocks * rows
            for s in (1, 2, 3):
                self.held[s] += (sizes[axes[s - 1]] - 1) * self.stride(axes, s) * rows

    def stride(self, axes, s):
        return math.prod(self.sizes[a] for a in axes[s:])


def span(start, size):
    return pl.ds(pl.multiple_of(start, 16), size)


def exchange_kernel(own, sizes, index_ref, tab, weight_ref, share_ref, full_ref, total_ref, *scratch):
    out_ref, coef_ref, pick, w_ref, share_out, share_in = scratch[:6]
    came, sums = scratch[6:10], (None,) + scratch[10:13]
    w_sem, sends, recvs, share_sends, share_recvs = scratch[13:]
    geo = Geometry(own, sizes)
    width = full_ref.shape[1]
    at = {a: lax.axis_index(a) for a in sizes}
    core = lax.axis_index("core")
    f32 = jnp.float32
    bf16 = jnp.bfloat16
    plan = geo.plan
    chunks = len(plan)

    loads = []
    for k, (rows, _) in enumerate(plan):
        part = pl.ds(geo.first[k], rows)
        loads.append(pltpu.make_async_copy(weight_ref.at[part], w_ref.at[part], w_sem.at[k]))
        loads[-1].start()

    def peer(axis, o):
        return {axis: lax.rem(at[axis] + o, sizes[axis])}

    peers = [{"core": 1 - core}]
    for axis, n in sizes.items():
        peers += [peer(axis, o) for o in range(1, n)]
    barrier = pltpu.get_barrier_semaphore()
    for p in peers:
        pl.semaphore_signal(barrier, inc=1, device_id=p, device_id_type=pl.DeviceIdType.MESH)
    started = []
    got = {}

    def send(stage, k, o, src, dst, to):
        copy = pltpu.make_async_remote_copy(
            src_ref=src,
            dst_ref=dst,
            send_sem=sends.at[stage, k, o - 1],
            recv_sem=recvs.at[stage, k, o - 1],
            device_id=to,
            device_id_type=pl.DeviceIdType.MESH,
        )
        copy.start()
        started.append(copy)
        return copy

    def arrive(stage, k):
        for copy in got[stage, k]:
            copy.wait_recv()

    def base_of(k, levels):
        axes = plan[k][1]
        return sum((at[axes[s - 1]] * geo.stride(axes, s) for s in range(1, levels + 1)), 0)

    def device_row(k, block, side):
        axes = plan[k][1]
        pos = {a: block // geo.stride(axes, s + 1) % sizes[a] for s, a in enumerate(axes)}
        chip = pos["z"] * sizes["x"] + pos["x"]
        return ((chip * 2 + side) * sizes["modes"] + pos["modes"]) * own + geo.first[k]

    def home(side, k, block):
        return side * geo.modes + geo.start[k][0] + block * plan[k][0]

    def partial(k, base, count, level):
        rows, axes = plan[k]
        total = coef_ref[span(home(core, k, base), count * rows)].astype(f32)
        total += came[0][span(home(0, k, base), count * rows)].astype(f32)
        inner = base
        for s in range(1, level + 1):
            stride = geo.stride(axes, s)
            inner = inner - at[axes[s - 1]] * stride
            for o in range(sizes[axes[s - 1]] - 1):
                lo = geo.start[k][s] + (o * stride + inner) * rows
                total += came[s][span(lo, count * rows)].astype(f32)
        return total

    def fetch(side, k):
        rows = plan[k][0]

        def body(block, carry):
            base = device_row(k, block, side)
            for i in range(rows):
                pick[pl.ds(2 * (block * rows + i), 2)] = tab[pl.ds(index_ref[base + i], 2)]
            return carry

        lax.fori_loop(0, geo.blocks, body, 0)
        count = geo.blocks * rows
        for half in range(2):
            part = pick[pl.ds(half, count, stride=2)].astype(bf16)
            coef_ref[span(home(side, k, 0), count), half * width : (half + 1) * width] = part

    def scatter0(k):
        if k > 0:
            fetch(1 - core, k)
        count = geo.blocks * plan[k][0]
        src = coef_ref.at[span(home(1 - core, k, 0), count)]
        got[0, k] = [send(0, k, 1, src, came[0].at[span(home(0, k, 0), count)], {"core": 1 - core})]
        if k > 0:
            fetch(core, k)

    def scatter(s):
        def run(k):
            arrive(s - 1, k)
            rows, axes = plan[k]
            axis, stride = axes[s - 1], geo.stride(axes, s)
            got[s, k] = []
            for o in range(1, sizes[axis]):
                to = peer(axis, o)
                slot = span(geo.start[k][s] + (o - 1) * stride * rows, stride * rows)
                sums[s][slot] = partial(k, base_of(k, s - 1) + to[axis] * stride, stride, s - 1).astype(bf16)
                got[s, k].append(send(s, k, o, sums[s].at[slot], came[s].at[slot], to))

        return run

    def mix(k):
        arrive(3, k)
        rows = plan[k][0]
        coef = partial(k, base_of(k, 3), 1, 3).astype(bf16)
        re, im = coef[:, :width], coef[:, width:]
        lhs = jnp.concatenate(
            [jnp.concatenate([re, -im], axis=1), jnp.concatenate([im, re], axis=1)], axis=0
        )
        ids = lax.rem(lax.broadcasted_iota(jnp.int32, (2 * rows, width), 0), rows)
        loads[k].wait()
        unroll = 16

        def body(step, acc):
            for i in range(unroll):
                m = step * unroll + i
                w = w_ref[geo.first[k] + m].reshape(2 * width, width)
                res = jnp.dot(lhs, w, preferred_element_type=f32)
                acc = jnp.where(ids == m, res, acc)
            return acc

        acc = lax.fori_loop(0, rows // unroll, body, jnp.zeros((2 * rows, width), f32))
        where = span(home(core, k, base_of(k, 3)), rows)
        out_ref[where, :width] = acc[:rows].astype(bf16)
        out_ref[where, width:] = acc[rows:].astype(bf16)

    def gather(s):
        def run(k):
            if s == 3:
                mix(k)
            else:
                arrive(7 - s - 1, k)
            rows, axes = plan[k]
            axis, stride = axes[s - 1], geo.stride(axes, s)
            where = out_ref.at[span(home(core, k, base_of(k, s)), stride * rows)]
            got[7 - s, k] = [send(7 - s, k, o, where, where, peer(axis, o)) for o in range(1, sizes[axis])]

        return run

    def gather0(k):
        arrive(6, k)
        where = out_ref.at[span(home(core, k, 0), geo.blocks * plan[k][0])]
        got[7, k] = [send(7, k, 1, where, where, {"core": 1 - core})]

    def expand(k):
        arrive(7, k)
        rows = plan[k][0]

        def body(block, carry):
            for side in range(2):
                to = 2 * device_row(k, block, side)
                values = out_ref[span(home(side, k, block), rows)].astype(f32)
                for half in range(2):
                    full_ref[pl.ds(to + half, rows, stride=2)] = values[:, half * width : (half + 1) * width]
            return carry

        lax.fori_loop(0, geo.blocks, body, 0)

    axes = (("core", 2),) + tuple(sizes.items())
    shares = {}

    def share_sum(level):
        value = share_out[level - 1]
        for o, copy in enumerate(shares[level - 1]):
            copy.wait_recv()
            value += share_in[level - 1, o]
        return value

    def share_step(level):
        axis, n = axes[level]
        share_out[level] = share_ref[...] if level == 0 else share_sum(level)
        shares[level] = []
        for o in range(1, n):
            copy = pltpu.make_async_remote_copy(
                src_ref=share_out.at[level],
                dst_ref=share_in.at[level, o - 1],
                send_sem=share_sends.at[level, o - 1],
                recv_sem=share_recvs.at[level, o - 1],
                device_id={"core": 1 - core} if level == 0 else peer(axis, o),
                device_id_type=pl.DeviceIdType.MESH,
            )
            copy.start()
            started.append(copy)
            shares[level].append(copy)

    for side in range(2):
        fetch(side, 0)
    pl.semaphore_wait(barrier, len(peers))
    stages = [scatter0, scatter(1), scatter(2), scatter(3), gather(3), gather(2), gather(1), gather0, expand]
    starts = [0] + [1 + 2 * s for s in range(len(stages) - 1)]
    for t in range(chunks + starts[-1]):
        for s in range(len(stages)):
            if 0 <= t - starts[s] < chunks:
                stages[s](t - starts[s])
        if t % 2 == 0 and t // 2 < len(axes):
            share_step(t // 2)
        elif t == 2 * len(axes):
            total_ref[...] = share_sum(len(axes))
    for copy in started:
        copy.wait_send()


def exchange(index, tab, weight, share, sizes):
    own, width = weight.shape[0], weight.shape[-1]
    geo = Geometry(own, sizes)
    chunks = len(geo.plan)
    hops = max(2, *sizes.values()) - 1
    held = [max(n, 16) for n in geo.held]

    def buf(n):
        return pltpu.VMEM((n, 2 * width), jnp.bfloat16)

    vmem = pl.BlockSpec(memory_space=pltpu.VMEM)
    return pl.pallas_call(
        functools.partial(exchange_kernel, own, sizes),
        out_shape=(jax.ShapeDtypeStruct(tab.shape, jnp.float32), jax.ShapeDtypeStruct(share.shape, jnp.float32)),
        in_specs=[pl.BlockSpec(memory_space=pltpu.SMEM), vmem, pl.BlockSpec(memory_space=pl.ANY), vmem],
        out_specs=(vmem, vmem),
        scratch_shapes=[
            buf(2 * geo.modes),
            buf(2 * geo.modes),
            pltpu.VMEM((2 * geo.blocks * max(rows for rows, _ in geo.plan) + PAD, width), jnp.float32),
            pltpu.VMEM(weight.shape, jnp.bfloat16),
            pltpu.VMEM((4,) + share.shape, jnp.float32),
            pltpu.VMEM((4, hops) + share.shape, jnp.float32),
            buf(held[0]), buf(held[1]), buf(held[2]), buf(held[3]),
            buf(held[1]), buf(held[2]), buf(held[3]),
            pltpu.SemaphoreType.DMA((chunks,)),
            pltpu.SemaphoreType.DMA((8, chunks, hops)),
            pltpu.SemaphoreType.DMA((8, chunks, hops)),
            pltpu.SemaphoreType.DMA((4, hops)),
            pltpu.SemaphoreType.DMA((4, hops)),
        ],
        compiler_params=pltpu.CompilerParams(
            collective_id=0, has_side_effects=True, vmem_limit_bytes=35 << 20
        ),
    )(index, tab, weight, share)


def grid_index(mode_table):
    kx = mode_table[0]
    slot = jnp.where(kx >= 0, kx, HALF - 1 - kx)
    return (slot * KY_COUNT + mode_table[1] - KY_LOW) * KZ_COUNT + mode_table[2] - KZ_LOW


def on_device(features, coords, quad_weight, mode_table, mode_weight, lin_weight, bias):
    sizes = {a: lax.axis_size(a) for a in ("x", "modes", "z")}
    rows = features.shape[0] // sizes["modes"]
    group = lax.axis_index("modes")[None]
    index = 2 * grid_index(mode_table)
    e, tab, xt, share = analyse(group, rows, coords, quad_weight[None, :], features, index)
    full, total = exchange(index, tab, mode_weight, share, sizes)
    return synthesize(index, group, e, xt, full, features, lin_weight, bias, total)


def solution(mesh):
    chips = mesh.shape["pts"] // 2
    n_x = 2 if chips % 2 == 0 else 1
    shape = (chips // n_x, n_x, 2, mesh.shape["modes"])
    mesh = Mesh(mesh.devices.reshape(shape), AXES)
    return jax.shard_map(
        on_device,
        mesh=mesh,
        in_specs=(
            P(PTS, None),
            P(None, PTS),
            P(PTS),
            P(),
            P(AXES, None, None, None),
            P(),
            P(),
        ),
        out_specs=P(AXES, None),
        check_vma=False,
    )
```

```python
import functools
import math

import jax
import jax.numpy as jnp
from jax import lax
from jax.experimental import pallas as pl
from jax.experimental.pallas import tpu as pltpu
from jax.sharding import Mesh
from jax.sharding import PartitionSpec as P

KX_LOW, KX_COUNT = -8, 16
KY_LOW, KY_COUNT = -8, 16
KZ_LOW, KZ_COUNT = 0, 32
HALF = KX_COUNT // 2
PLANE = KY_COUNT * KZ_COUNT
PTS = ("z", "x", "core")
AXES = PTS + ("modes",)
PAD = 8


def product(a, b):
    return a[0] * b[0] - a[1] * b[1], a[0] * b[1] + a[1] * b[0]


def powers(out_c, out_s, start, unit, count):
    out_c[0:1], out_s[0:1] = start
    n = 1
    while n < count:
        out_c[n : 2 * n], out_s[n : 2 * n] = product((out_c[0:n], out_s[0:n]), unit)
        unit = product(unit, unit)
        n *= 2
    return unit


def analyse_kernel(coords_ref, features_ref, *refs):
    e_ref, tab, xt_ref, share_ref, weighted, yc, ys, zc, zs = refs[-9:]
    j = pl.program_id(0)
    width = weighted.shape[0]
    bf16 = jnp.bfloat16

    @pl.when(j == 0)
    def _():
        base, quad = coords_ref[0:3], coords_ref[3:4]
        turns = jnp.concatenate([0.5 * base[0:1], base[1:3]], axis=0)
        angle = (2.0 * math.pi) * (turns - jnp.round(turns))
        cos, sin = jnp.cos(angle), jnp.sin(angle)
        half, y, z = ((cos[i : i + 1], sin[i : i + 1]) for i in range(3))
        powers(xt_ref.at[:HALF], xt_ref.at[HALF:], half, product(half, half), HALF)
        one = jnp.ones_like(half[0])
        mid = KY_COUNT // 2
        far = powers(yc.at[mid:], ys.at[mid:], (one, 0.0 * one), y, mid)
        far = (far[0], -far[1])
        yc[:mid], ys[:mid] = product((yc[mid:], ys[mid:]), far)
        powers(zc, zs, (half[0], -half[1]), z, KZ_COUNT)
        for k in range(KY_COUNT):
            re, im = product((yc[k : k + 1], ys[k : k + 1]), (zc[...], zs[...]))
            e_ref[pl.ds(k * KZ_COUNT, KZ_COUNT)] = re.astype(bf16)
            e_ref[pl.ds(PLANE + k * KZ_COUNT, KZ_COUNT)] = im.astype(bf16)
        share_ref[...] = jnp.broadcast_to(jnp.sum(quad, axis=1, keepdims=True), share_ref.shape)
        scaled = quad * features_ref[...].astype(jnp.float32).T
        weighted[...] = scaled.astype(bf16).astype(jnp.float32)

    by_cos = (xt_ref[pl.ds(j, 1)] * weighted[...]).astype(bf16)
    by_sin = (xt_ref[pl.ds(HALF + j, 1)] * weighted[...]).astype(bf16)
    rhs = jnp.concatenate([by_cos, by_sin], axis=0)
    dims = (((1,), (1,)), ((), ()))
    re = lax.dot_general(e_ref[:PLANE], rhs, dims, preferred_element_type=jnp.float32)
    im = lax.dot_general(e_ref[PLANE:], rhs, dims, preferred_element_type=jnp.float32)
    rc, rs = re[:, :width], re[:, width:]
    ic, is_ = im[:, :width], im[:, width:]
    pos = pl.multiple_of(2 * j * PLANE, 2 * PLANE)
    neg = pl.multiple_of(2 * (HALF + j) * PLANE, 2 * PLANE)
    tab[pl.ds(pos, PLANE, stride=2)] = rc - is_
    tab[pl.ds(pos + 1, PLANE, stride=2)] = -(ic + rs)
    tab[pl.ds(neg, PLANE, stride=2)] = rc + is_
    tab[pl.ds(neg + 1, PLANE, stride=2)] = rs - ic


def analyse(coords, features, *after):
    rows, width = features.shape
    f32 = jnp.float32
    whole = pl.BlockSpec(memory_space=pltpu.VMEM)
    return pl.pallas_call(
        analyse_kernel,
        out_shape=(
            jax.ShapeDtypeStruct((2 * PLANE, rows), jnp.bfloat16),
            jax.ShapeDtypeStruct((4 * HALF * PLANE + PAD, width), f32),
            jax.ShapeDtypeStruct((2 * HALF, rows), f32),
            jax.ShapeDtypeStruct((8, width), f32),
        ),
        grid=(HALF,),
        in_specs=[whole, whole] + [pl.BlockSpec(memory_space=pl.ANY)] * len(after),
        out_specs=(whole,) * 4,
        scratch_shapes=[pltpu.VMEM((width, rows), f32)]
        + [pltpu.VMEM((n, rows), f32) for n in (KY_COUNT, KY_COUNT, KZ_COUNT, KZ_COUNT)],
        compiler_params=pltpu.CompilerParams(vmem_limit_bytes=16 << 20),
    )(coords, features, *after)


def synthesize_kernel(
    order_ref, e_ref, xt_ref, full_ref, features_ref, lin_ref, bias_ref, total_ref, out_ref, tab, acc
):
    j = pl.program_id(0)
    width = out_ref.shape[1]
    f32 = jnp.float32

    @pl.when(j == 0)
    def _():
        unroll = math.gcd(full_ref.shape[0] // 2 - PAD // 2, 128)

        @pl.loop(0, full_ref.shape[0] // (2 * unroll))
        def _(block):
            for i in range(unroll):
                q = block * unroll + i
                tab[pl.ds(pl.multiple_of(order_ref[q], 2), 2)] = full_ref[pl.ds(pl.multiple_of(2 * q, 2), 2)]

        acc[...] = jnp.zeros_like(acc)

    pos = pl.multiple_of(2 * j * PLANE, 2 * PLANE)
    neg = pl.multiple_of(2 * (HALF + j) * PLANE, 2 * PLANE)
    pr, pi, nr, ni = (tab[pl.ds(at, PLANE, stride=2)] for at in (pos, pos + 1, neg, neg + 1))
    top = jnp.concatenate([pr + nr, ni - pi], axis=1).astype(jnp.bfloat16)
    low = jnp.concatenate([-(pi + ni), nr - pr], axis=1).astype(jnp.bfloat16)
    rhs = jnp.concatenate([top, low], axis=0)
    dims = (((0,), (0,)), ((), ()))
    field = lax.dot_general(rhs, e_ref[...], dims, preferred_element_type=f32)
    acc[...] += xt_ref[pl.ds(j, 1)] * field[:width] + xt_ref[pl.ds(HALF + j, 1)] * field[width:]

    @pl.when(j == pl.num_programs(0) - 1)
    def _():
        linear = jnp.dot(features_ref[...], lin_ref[...], preferred_element_type=f32)
        pre = acc[...].T * (1.0 / total_ref[0:1]) + linear + bias_ref[...]
        out_ref[...] = (0.5 * pre * (1.0 + lax.erf(pre * math.sqrt(0.5)))).astype(out_ref.dtype)


def synthesize(order, e, xt, full, features, lin_weight, bias, total):
    rows, width = e.shape[1], features.shape[1]
    whole = pl.BlockSpec(memory_space=pltpu.VMEM)
    return pl.pallas_call(
        synthesize_kernel,
        out_shape=jax.ShapeDtypeStruct((rows, width), jnp.bfloat16),
        grid_spec=pltpu.PrefetchScalarGridSpec(
            num_scalar_prefetch=1,
            grid=(HALF,),
            in_specs=[whole] * 7,
            out_specs=pl.BlockSpec((rows, width), lambda j, order: (0, 0)),
            scratch_shapes=[pltpu.VMEM(full.shape, jnp.float32), pltpu.VMEM((width, rows), jnp.float32)],
        ),
        compiler_params=pltpu.CompilerParams(vmem_limit_bytes=16 << 20),
    )(order, e, xt, full, features, lin_weight, bias[None, :], total)


def chunk_plan(own):
    axes = ("x", "modes", "z"), ("modes", "x", "z")
    chunks = max(2, min(8, own // 16))
    return [(own // chunks, axes[k % 2]) for k in range(chunks)]


class Geometry:
    def __init__(self, own, sizes):
        self.sizes = sizes
        self.plan = chunk_plan(own)
        self.blocks = math.prod(sizes.values())
        self.modes = self.blocks * own
        self.first, self.start = [], []
        self.held = [0] * 4
        done = 0
        for rows, axes in self.plan:
            self.first.append(done)
            done += rows
            self.start.append(list(self.held))
            self.held[0] += self.blocks * rows
            for s in (1, 2, 3):
                self.held[s] += (sizes[axes[s - 1]] - 1) * self.stride(axes, s) * rows

    def stride(self, axes, s):
        return math.prod(self.sizes[a] for a in axes[s:])


def span(start, size):
    return pl.ds(pl.multiple_of(start, 16), size)


def exchange_kernel(own, sizes, index_ref, tab, weight_ref, share_ref, full_ref, total_ref, *scratch):
    out_ref, coef_ref, pick, w_ref, share_out, share_in = scratch[:6]
    came, sums = scratch[6:10], (None,) + scratch[10:13]
    w_sem, sends, recvs, share_sends, share_recvs = scratch[13:]
    geo = Geometry(own, sizes)
    width = full_ref.shape[1]
    at = {a: lax.axis_index(a) for a in sizes}
    core = lax.axis_index("core")
    f32 = jnp.float32
    bf16 = jnp.bfloat16
    plan = geo.plan
    chunks = len(plan)

    loads = []
    for k, (rows, _) in enumerate(plan):
        part = pl.ds(geo.first[k], rows)
        loads.append(pltpu.make_async_copy(weight_ref.at[part], w_ref.at[part], w_sem.at[k]))
        loads[-1].start()

    def peer(axis, o):
        return {axis: lax.rem(at[axis] + o, sizes[axis])}

    peers = [{"core": 1 - core}]
    for axis, n in sizes.items():
        peers += [peer(axis, o) for o in range(1, n)]
    barrier = pltpu.get_barrier_semaphore()
    for p in peers:
        pl.semaphore_signal(barrier, inc=1, device_id=p, device_id_type=pl.DeviceIdType.MESH)
    started = []
    got = {}

    def send(stage, k, o, src, dst, to):
        copy = pltpu.make_async_remote_copy(
            src_ref=src,
            dst_ref=dst,
            send_sem=sends.at[stage, k, o - 1],
            recv_sem=recvs.at[stage, k, o - 1],
            device_id=to,
            device_id_type=pl.DeviceIdType.MESH,
        )
        copy.start()
        started.append(copy)
        return copy

    def arrive(stage, k):
        for copy in got[stage, k]:
            copy.wait_recv()

    def base_of(k, levels):
        axes = plan[k][1]
        return sum((at[axes[s - 1]] * geo.stride(axes, s) for s in range(1, levels + 1)), 0)

    def device_row(k, block, side):
        axes = plan[k][1]
        pos = {a: block // geo.stride(axes, s + 1) % sizes[a] for s, a in enumerate(axes)}
        chip = pos["z"] * sizes["x"] + pos["x"]
        return ((chip * 2 + side) * sizes["modes"] + pos["modes"]) * own + geo.first[k]

    def home(side, k, block):
        return side * geo.modes + geo.start[k][0] + block * plan[k][0]

    def partial(k, base, count, level):
        rows, axes = plan[k]
        total = coef_ref[span(home(core, k, base), count * rows)].astype(f32)
        total += came[0][span(home(0, k, base), count * rows)].astype(f32)
        inner = base
        for s in range(1, level + 1):
            stride = geo.stride(axes, s)
            inner = inner - at[axes[s - 1]] * stride
            for o in range(sizes[axes[s - 1]] - 1):
                lo = geo.start[k][s] + (o * stride + inner) * rows
                total += came[s][span(lo, count * rows)].astype(f32)
        return total

    def fetch(side, k):
        rows = plan[k][0]

        def body(block, carry):
            base = device_row(k, block, side)
            for i in range(rows):
                pick[pl.ds(2 * (block * rows + i), 2)] = tab[pl.ds(index_ref[base + i], 2)]
            return carry

        lax.fori_loop(0, geo.blocks, body, 0)
        count = geo.blocks * rows
        for half in range(2):
            part = pick[pl.ds(half, count, stride=2)].astype(bf16)
            coef_ref[span(home(side, k, 0), count), half * width : (half + 1) * width] = part

    def scatter0(k):
        if k > 0:
            fetch(1 - core, k)
        count = geo.blocks * plan[k][0]
        src = coef_ref.at[span(home(1 - core, k, 0), count)]
        got[0, k] = [send(0, k, 1, src, came[0].at[span(home(0, k, 0), count)], {"core": 1 - core})]
        if k > 0:
            fetch(core, k)

    def scatter(s):
        def run(k):
            arrive(s - 1, k)
            rows, axes = plan[k]
            axis, stride = axes[s - 1], geo.stride(axes, s)
            got[s, k] = []
            for o in range(1, sizes[axis]):
                to = peer(axis, o)
                slot = span(geo.start[k][s] + (o - 1) * stride * rows, stride * rows)
                sums[s][slot] = partial(k, base_of(k, s - 1) + to[axis] * stride, stride, s - 1).astype(bf16)
                got[s, k].append(send(s, k, o, sums[s].at[slot], came[s].at[slot], to))

        return run

    def mix(k):
        arrive(3, k)
        rows = plan[k][0]
        coef = partial(k, base_of(k, 3), 1, 3).astype(bf16)
        re, im = coef[:, :width], coef[:, width:]
        lhs = jnp.concatenate(
            [jnp.concatenate([re, -im], axis=1), jnp.concatenate([im, re], axis=1)], axis=0
        )
        ids = lax.rem(lax.broadcasted_iota(jnp.int32, (2 * rows, width), 0), rows)
        loads[k].wait()
        unroll = 16

        def body(step, acc):
            for i in range(unroll):
                m = step * unroll + i
                w = w_ref[geo.first[k] + m].reshape(2 * width, width)
                res = jnp.dot(lhs, w, preferred_element_type=f32)
                acc = jnp.where(ids == m, res, acc)
            return acc

        acc = lax.fori_loop(0, rows // unroll, body, jnp.zeros((2 * rows, width), f32))
        where = span(home(core, k, base_of(k, 3)), rows)
        out_ref[where, :width] = acc[:rows].astype(bf16)
        out_ref[where, width:] = acc[rows:].astype(bf16)

    def gather(s):
        def run(k):
            if s == 3:
                mix(k)
            else:
                arrive(7 - s - 1, k)
            rows, axes = plan[k]
            axis, stride = axes[s - 1], geo.stride(axes, s)
            where = out_ref.at[span(home(core, k, base_of(k, s)), stride * rows)]
            got[7 - s, k] = [send(7 - s, k, o, where, where, peer(axis, o)) for o in range(1, sizes[axis])]

        return run

    def gather0(k):
        arrive(6, k)
        where = out_ref.at[span(home(core, k, 0), geo.blocks * plan[k][0])]
        got[7, k] = [send(7, k, 1, where, where, {"core": 1 - core})]

    def expand(k):
        arrive(7, k)
        rows = plan[k][0]

        def body(block, carry):
            for side in range(2):
                to = 2 * device_row(k, block, side)
                values = out_ref[span(home(side, k, block), rows)].astype(f32)
                for half in range(2):
                    full_ref[pl.ds(to + half, rows, stride=2)] = values[:, half * width : (half + 1) * width]
            return carry

        lax.fori_loop(0, geo.blocks, body, 0)

    axes = (("core", 2),) + tuple(sizes.items())
    shares = {}

    def share_sum(level):
        value = share_out[level - 1]
        for o, copy in enumerate(shares[level - 1]):
            copy.wait_recv()
            value += share_in[level - 1, o]
        return value

    def share_step(level):
        axis, n = axes[level]
        share_out[level] = share_ref[...] if level == 0 else share_sum(level)
        shares[level] = []
        for o in range(1, n):
            copy = pltpu.make_async_remote_copy(
                src_ref=share_out.at[level],
                dst_ref=share_in.at[level, o - 1],
                send_sem=share_sends.at[level, o - 1],
                recv_sem=share_recvs.at[level, o - 1],
                device_id={"core": 1 - core} if level == 0 else peer(axis, o),
                device_id_type=pl.DeviceIdType.MESH,
            )
            copy.start()
            started.append(copy)
            shares[level].append(copy)

    for side in range(2):
        fetch(side, 0)
    pl.semaphore_wait(barrier, len(peers))
    stages = [scatter0, scatter(1), scatter(2), scatter(3), gather(3), gather(2), gather(1), gather0, expand]
    starts = [0] + [1 + 2 * s for s in range(len(stages) - 1)]
    for t in range(chunks + starts[-1]):
        for s in range(len(stages)):
            if 0 <= t - starts[s] < chunks:
                stages[s](t - starts[s])
        if t % 2 == 0 and t // 2 < len(axes):
            share_step(t // 2)
        elif t == 2 * len(axes):
            total_ref[...] = share_sum(len(axes))
    for copy in started:
        copy.wait_send()


def exchange(index, tab, weight, share, sizes):
    own, width = weight.shape[0], weight.shape[-1]
    geo = Geometry(own, sizes)
    chunks = len(geo.plan)
    hops = max(2, *sizes.values()) - 1
    held = [max(n, 16) for n in geo.held]

    def buf(n):
        return pltpu.VMEM((n, 2 * width), jnp.bfloat16)

    vmem = pl.BlockSpec(memory_space=pltpu.VMEM)
    return pl.pallas_call(
        functools.partial(exchange_kernel, own, sizes),
        out_shape=(jax.ShapeDtypeStruct(tab.shape, jnp.float32), jax.ShapeDtypeStruct(share.shape, jnp.float32)),
        in_specs=[pl.BlockSpec(memory_space=pltpu.SMEM), vmem, pl.BlockSpec(memory_space=pl.ANY), vmem],
        out_specs=(vmem, vmem),
        scratch_shapes=[
            buf(2 * geo.modes),
            buf(2 * geo.modes),
            pltpu.VMEM((2 * geo.blocks * max(rows for rows, _ in geo.plan) + PAD, width), jnp.float32),
            pltpu.VMEM(weight.shape, jnp.bfloat16),
            pltpu.VMEM((4,) + share.shape, jnp.float32),
            pltpu.VMEM((4, hops) + share.shape, jnp.float32),
            buf(held[0]), buf(held[1]), buf(held[2]), buf(held[3]),
            buf(held[1]), buf(held[2]), buf(held[3]),
            pltpu.SemaphoreType.DMA((chunks,)),
            pltpu.SemaphoreType.DMA((8, chunks, hops)),
            pltpu.SemaphoreType.DMA((8, chunks, hops)),
            pltpu.SemaphoreType.DMA((4, hops)),
            pltpu.SemaphoreType.DMA((4, hops)),
        ],
        compiler_params=pltpu.CompilerParams(
            collective_id=0, has_side_effects=True, vmem_limit_bytes=35 << 20
        ),
    )(index, tab, weight, share)


def grid_index(mode_table):
    kx = mode_table[0]
    slot = jnp.where(kx >= 0, kx, HALF - 1 - kx)
    return (slot * KY_COUNT + mode_table[1] - KY_LOW) * KZ_COUNT + mode_table[2] - KZ_LOW


def on_device(features, coords, quad_weight, mode_table, mode_weight, lin_weight, bias):
    sizes = {a: lax.axis_size(a) for a in ("x", "modes", "z")}
    rows = features.shape[0] // sizes["modes"]
    start = lax.axis_index("modes") * rows
    features = lax.dynamic_slice_in_dim(features, start, rows, 0)
    table = jnp.concatenate([coords, quad_weight[None, :]], axis=0)
    table = lax.dynamic_slice_in_dim(table, start, rows, 1)
    index = 2 * grid_index(mode_table)
    e, tab, xt, share = analyse(table, features, index)
    full, total = exchange(index, tab, mode_weight, share, sizes)
    return synthesize(index, e, xt, full, features, lin_weight, bias, total)


def solution(mesh):
    chips = mesh.shape["pts"] // 2
    n_x = 2 if chips % 2 == 0 else 1
    shape = (chips // n_x, n_x, 2, mesh.shape["modes"])
    mesh = Mesh(mesh.devices.reshape(shape), AXES)
    return jax.shard_map(
        on_device,
        mesh=mesh,
        in_specs=(
            P(PTS, None),
            P(None, PTS),
            P(PTS),
            P(),
            P(AXES, None, None, None),
            P(),
            P(),
        ),
        out_specs=P(AXES, None),
        check_vma=False,
    )
```

```python
import functools
import math

import jax
import jax.numpy as jnp
from jax import lax
from jax.experimental import pallas as pl
from jax.experimental.pallas import tpu as pltpu
from jax.sharding import Mesh
from jax.sharding import PartitionSpec as P

KX_LOW, KX_COUNT = -8, 16
KY_LOW, KY_COUNT = -8, 16
KZ_LOW, KZ_COUNT = 0, 32
HALF = KX_COUNT // 2
PLANE = KY_COUNT * KZ_COUNT
PTS = ("z", "x", "core")
AXES = PTS + ("modes",)
PAD = 8


def product(a, b):
    return a[0] * b[0] - a[1] * b[1], a[0] * b[1] + a[1] * b[0]


def powers(out_c, out_s, start, unit, count):
    out_c[0:1], out_s[0:1] = start
    n = 1
    while n < count:
        out_c[n : 2 * n], out_s[n : 2 * n] = product((out_c[0:n], out_s[0:n]), unit)
        unit = product(unit, unit)
        n *= 2
    return unit


def analyse_kernel(coords_ref, features_ref, *refs):
    e_ref, tab, xt_ref, share_ref, weighted, yc, ys, zc, zs = refs[-9:]
    j = pl.program_id(0)
    width = weighted.shape[0]
    bf16 = jnp.bfloat16

    @pl.when(j == 0)
    def _():
        base, quad = coords_ref[0:3], coords_ref[3:4]
        turns = jnp.concatenate([0.5 * base[0:1], base[1:3]], axis=0)
        angle = (2.0 * math.pi) * (turns - jnp.round(turns))
        cos, sin = jnp.cos(angle), jnp.sin(angle)
        half, y, z = ((cos[i : i + 1], sin[i : i + 1]) for i in range(3))
        powers(xt_ref.at[:HALF], xt_ref.at[HALF:], half, product(half, half), HALF)
        one = jnp.ones_like(half[0])
        mid = KY_COUNT // 2
        far = powers(yc.at[mid:], ys.at[mid:], (one, 0.0 * one), y, mid)
        far = (far[0], -far[1])
        yc[:mid], ys[:mid] = product((yc[mid:], ys[mid:]), far)
        powers(zc, zs, (half[0], -half[1]), z, KZ_COUNT)

        def put(k, re, im):
            e_ref[pl.ds(k * KZ_COUNT, KZ_COUNT)] = re.astype(bf16)
            e_ref[pl.ds(PLANE + k * KZ_COUNT, KZ_COUNT)] = im.astype(bf16)

        put(mid, zc[...], zs[...])
        put(0, *product((yc[0:1], ys[0:1]), (zc[...], zs[...])))
        for k in range(1, mid):
            c, s = yc[mid + k : mid + k + 1], ys[mid + k : mid + k + 1]
            cc, ss, cs, sc = c * zc[...], s * zs[...], c * zs[...], s * zc[...]
            put(mid + k, cc - ss, cs + sc)
            put(mid - k, cc + ss, cs - sc)
        share_ref[...] = jnp.broadcast_to(jnp.sum(quad, axis=1, keepdims=True), share_ref.shape)
        scaled = quad * features_ref[...].astype(jnp.float32).T
        weighted[...] = scaled.astype(bf16).astype(jnp.float32)

    by_cos = (xt_ref[pl.ds(j, 1)] * weighted[...]).astype(bf16)
    by_sin = (xt_ref[pl.ds(HALF + j, 1)] * weighted[...]).astype(bf16)
    rhs = jnp.concatenate([by_cos, by_sin], axis=0)
    dims = (((1,), (1,)), ((), ()))
    re = lax.dot_general(e_ref[:PLANE], rhs, dims, preferred_element_type=jnp.float32)
    im = lax.dot_general(e_ref[PLANE:], rhs, dims, preferred_element_type=jnp.float32)
    rc, rs = re[:, :width], re[:, width:]
    ic, is_ = im[:, :width], im[:, width:]
    pos = pl.multiple_of(2 * j * PLANE, 2 * PLANE)
    neg = pl.multiple_of(2 * (HALF + j) * PLANE, 2 * PLANE)
    tab[pl.ds(pos, PLANE, stride=2)] = rc - is_
    tab[pl.ds(pos + 1, PLANE, stride=2)] = -(ic + rs)
    tab[pl.ds(neg, PLANE, stride=2)] = rc + is_
    tab[pl.ds(neg + 1, PLANE, stride=2)] = rs - ic


def analyse(coords, features, *after):
    rows, width = features.shape
    f32 = jnp.float32
    whole = pl.BlockSpec(memory_space=pltpu.VMEM)
    return pl.pallas_call(
        analyse_kernel,
        out_shape=(
            jax.ShapeDtypeStruct((2 * PLANE, rows), jnp.bfloat16),
            jax.ShapeDtypeStruct((4 * HALF * PLANE + PAD, width), f32),
            jax.ShapeDtypeStruct((2 * HALF, rows), f32),
            jax.ShapeDtypeStruct((8, width), f32),
        ),
        grid=(HALF,),
        in_specs=[whole, whole] + [pl.BlockSpec(memory_space=pl.ANY)] * len(after),
        out_specs=(whole,) * 4,
        scratch_shapes=[pltpu.VMEM((width, rows), f32)]
        + [pltpu.VMEM((n, rows), f32) for n in (KY_COUNT, KY_COUNT, KZ_COUNT, KZ_COUNT)],
        compiler_params=pltpu.CompilerParams(vmem_limit_bytes=16 << 20),
    )(coords, features, *after)


def synthesize_kernel(
    order_ref, e_ref, xt_ref, full_ref, features_ref, lin_ref, bias_ref, total_ref, out_ref, tab, acc
):
    j = pl.program_id(0)
    width = out_ref.shape[1]
    f32 = jnp.float32

    @pl.when(j == 0)
    def _():
        unroll = math.gcd(full_ref.shape[0] // 2 - PAD // 2, 128)

        @pl.loop(0, full_ref.shape[0] // (2 * unroll))
        def _(block):
            for i in range(unroll):
                q = block * unroll + i
                tab[pl.ds(pl.multiple_of(order_ref[q], 2), 2)] = full_ref[pl.ds(pl.multiple_of(2 * q, 2), 2)]

        acc[...] = jnp.zeros_like(acc)

    pos = pl.multiple_of(2 * j * PLANE, 2 * PLANE)
    neg = pl.multiple_of(2 * (HALF + j) * PLANE, 2 * PLANE)
    pr, pi, nr, ni = (tab[pl.ds(at, PLANE, stride=2)] for at in (pos, pos + 1, neg, neg + 1))
    top = jnp.concatenate([pr + nr, ni - pi], axis=1).astype(jnp.bfloat16)
    low = jnp.concatenate([-(pi + ni), nr - pr], axis=1).astype(jnp.bfloat16)
    rhs = jnp.concatenate([top, low], axis=0)
    dims = (((0,), (0,)), ((), ()))
    field = lax.dot_general(rhs, e_ref[...], dims, preferred_element_type=f32)
    acc[...] += xt_ref[pl.ds(j, 1)] * field[:width] + xt_ref[pl.ds(HALF + j, 1)] * field[width:]

    @pl.when(j == pl.num_programs(0) - 1)
    def _():
        linear = jnp.dot(features_ref[...], lin_ref[...], preferred_element_type=f32)
        pre = acc[...].T * (1.0 / total_ref[0:1]) + linear + bias_ref[...]
        out_ref[...] = (0.5 * pre * (1.0 + lax.erf(pre * math.sqrt(0.5)))).astype(out_ref.dtype)


def synthesize(order, e, xt, full, features, lin_weight, bias, total):
    rows, width = e.shape[1], features.shape[1]
    whole = pl.BlockSpec(memory_space=pltpu.VMEM)
    return pl.pallas_call(
        synthesize_kernel,
        out_shape=jax.ShapeDtypeStruct((rows, width), jnp.bfloat16),
        grid_spec=pltpu.PrefetchScalarGridSpec(
            num_scalar_prefetch=1,
            grid=(HALF,),
            in_specs=[whole] * 7,
            out_specs=pl.BlockSpec((rows, width), lambda j, order: (0, 0)),
            scratch_shapes=[pltpu.VMEM(full.shape, jnp.float32), pltpu.VMEM((width, rows), jnp.float32)],
        ),
        compiler_params=pltpu.CompilerParams(vmem_limit_bytes=16 << 20),
    )(order, e, xt, full, features, lin_weight, bias[None, :], total)


def chunk_plan(own):
    axes = ("x", "modes", "z"), ("modes", "x", "z")
    chunks = max(2, min(8, own // 16))
    return [(own // chunks, axes[k % 2]) for k in range(chunks)]


class Geometry:
    def __init__(self, own, sizes):
        self.sizes = sizes
        self.plan = chunk_plan(own)
        self.blocks = math.prod(sizes.values())
        self.modes = self.blocks * own
        self.first, self.start = [], []
        self.held = [0] * 4
        done = 0
        for rows, axes in self.plan:
            self.first.append(done)
            done += rows
            self.start.append(list(self.held))
            self.held[0] += self.blocks * rows
            for s in (1, 2, 3):
                self.held[s] += (sizes[axes[s - 1]] - 1) * self.stride(axes, s) * rows

    def stride(self, axes, s):
        return math.prod(self.sizes[a] for a in axes[s:])


def span(start, size):
    return pl.ds(pl.multiple_of(start, 16), size)


def exchange_kernel(own, sizes, index_ref, tab, weight_ref, share_ref, full_ref, total_ref, *scratch):
    out_ref, coef_ref, pick, w_ref, share_out, share_in = scratch[:6]
    came, sums = scratch[6:10], (None,) + scratch[10:13]
    w_sem, sends, recvs, share_sends, share_recvs = scratch[13:]
    geo = Geometry(own, sizes)
    width = full_ref.shape[1]
    at = {a: lax.axis_index(a) for a in sizes}
    core = lax.axis_index("core")
    f32 = jnp.float32
    bf16 = jnp.bfloat16
    plan = geo.plan
    chunks = len(plan)

    loads = []
    for k, (rows, _) in enumerate(plan):
        part = pl.ds(geo.first[k], rows)
        loads.append(pltpu.make_async_copy(weight_ref.at[part], w_ref.at[part], w_sem.at[k]))
        loads[-1].start()

    def peer(axis, o):
        return {axis: lax.rem(at[axis] + o, sizes[axis])}

    peers = [{"core": 1 - core}]
    for axis, n in sizes.items():
        peers += [peer(axis, o) for o in range(1, n)]
    barrier = pltpu.get_barrier_semaphore()
    for p in peers:
        pl.semaphore_signal(barrier, inc=1, device_id=p, device_id_type=pl.DeviceIdType.MESH)
    started = []
    got = {}

    def send(stage, k, o, src, dst, to):
        copy = pltpu.make_async_remote_copy(
            src_ref=src,
            dst_ref=dst,
            send_sem=sends.at[stage, k, o - 1],
            recv_sem=recvs.at[stage, k, o - 1],
            device_id=to,
            device_id_type=pl.DeviceIdType.MESH,
        )
        copy.start()
        started.append(copy)
        return copy

    def arrive(stage, k):
        for copy in got[stage, k]:
            copy.wait_recv()

    def base_of(k, levels):
        axes = plan[k][1]
        return sum((at[axes[s - 1]] * geo.stride(axes, s) for s in range(1, levels + 1)), 0)

    def device_row(k, block, side):
        axes = plan[k][1]
        pos = {a: block // geo.stride(axes, s + 1) % sizes[a] for s, a in enumerate(axes)}
        chip = pos["z"] * sizes["x"] + pos["x"]
        return ((chip * 2 + side) * sizes["modes"] + pos["modes"]) * own + geo.first[k]

    def home(side, k, block):
        return side * geo.modes + geo.start[k][0] + block * plan[k][0]

    def partial(k, base, count, level):
        rows, axes = plan[k]
        total = coef_ref[span(home(core, k, base), count * rows)].astype(f32)
        total += came[0][span(home(0, k, base), count * rows)].astype(f32)
        inner = base
        for s in range(1, level + 1):
            stride = geo.stride(axes, s)
            inner = inner - at[axes[s - 1]] * stride
            for o in range(sizes[axes[s - 1]] - 1):
                lo = geo.start[k][s] + (o * stride + inner) * rows
                total += came[s][span(lo, count * rows)].astype(f32)
        return total

    def fetch(side, k):
        rows = plan[k][0]

        def body(block, carry):
            base = device_row(k, block, side)
            for i in range(rows):
                pick[pl.ds(2 * (block * rows + i), 2)] = tab[pl.ds(index_ref[base + i], 2)]
            return carry

        lax.fori_loop(0, geo.blocks, body, 0)
        count = geo.blocks * rows
        for half in range(2):
            part = pick[pl.ds(half, count, stride=2)].astype(bf16)
            coef_ref[span(home(side, k, 0), count), half * width : (half + 1) * width] = part

    def scatter0(k):
        if k > 0:
            fetch(1 - core, k)
        count = geo.blocks * plan[k][0]
        src = coef_ref.at[span(home(1 - core, k, 0), count)]
        got[0, k] = [send(0, k, 1, src, came[0].at[span(home(0, k, 0), count)], {"core": 1 - core})]
        if k > 0:
            fetch(core, k)

    def scatter(s):
        def run(k):
            arrive(s - 1, k)
            rows, axes = plan[k]
            axis, stride = axes[s - 1], geo.stride(axes, s)
            got[s, k] = []
            for o in range(1, sizes[axis]):
                to = peer(axis, o)
                slot = span(geo.start[k][s] + (o - 1) * stride * rows, stride * rows)
                sums[s][slot] = partial(k, base_of(k, s - 1) + to[axis] * stride, stride, s - 1).astype(bf16)
                got[s, k].append(send(s, k, o, sums[s].at[slot], came[s].at[slot], to))

        return run

    def mix(k):
        arrive(3, k)
        rows = plan[k][0]
        coef = partial(k, base_of(k, 3), 1, 3).astype(bf16)
        re, im = coef[:, :width], coef[:, width:]
        lhs = jnp.concatenate(
            [jnp.concatenate([re, -im], axis=1), jnp.concatenate([im, re], axis=1)], axis=0
        )
        ids = lax.rem(lax.broadcasted_iota(jnp.int32, (2 * rows, width), 0), rows)
        loads[k].wait()
        unroll = 16

        def body(step, acc):
            for i in range(unroll):
                m = step * unroll + i
                w = w_ref[geo.first[k] + m].reshape(2 * width, width)
                res = jnp.dot(lhs, w, preferred_element_type=f32)
                acc = jnp.where(ids == m, res, acc)
            return acc

        acc = lax.fori_loop(0, rows // unroll, body, jnp.zeros((2 * rows, width), f32))
        where = span(home(core, k, base_of(k, 3)), rows)
        out_ref[where, :width] = acc[:rows].astype(bf16)
        out_ref[where, width:] = acc[rows:].astype(bf16)

    def gather(s):
        def run(k):
            if s == 3:
                mix(k)
            else:
                arrive(7 - s - 1, k)
            rows, axes = plan[k]
            axis, stride = axes[s - 1], geo.stride(axes, s)
            where = out_ref.at[span(home(core, k, base_of(k, s)), stride * rows)]
            got[7 - s, k] = [send(7 - s, k, o, where, where, peer(axis, o)) for o in range(1, sizes[axis])]

        return run

    def gather0(k):
        arrive(6, k)
        where = out_ref.at[span(home(core, k, 0), geo.blocks * plan[k][0])]
        got[7, k] = [send(7, k, 1, where, where, {"core": 1 - core})]

    def expand(k):
        arrive(7, k)
        rows = plan[k][0]

        def body(block, carry):
            for side in range(2):
                to = 2 * device_row(k, block, side)
                values = out_ref[span(home(side, k, block), rows)].astype(f32)
                for half in range(2):
                    full_ref[pl.ds(to + half, rows, stride=2)] = values[:, half * width : (half + 1) * width]
            return carry

        lax.fori_loop(0, geo.blocks, body, 0)

    axes = (("core", 2),) + tuple(sizes.items())
    shares = {}

    def share_sum(level):
        value = share_out[level - 1]
        for o, copy in enumerate(shares[level - 1]):
            copy.wait_recv()
            value += share_in[level - 1, o]
        return value

    def share_step(level):
        axis, n = axes[level]
        share_out[level] = share_ref[...] if level == 0 else share_sum(level)
        shares[level] = []
        for o in range(1, n):
            copy = pltpu.make_async_remote_copy(
                src_ref=share_out.at[level],
                dst_ref=share_in.at[level, o - 1],
                send_sem=share_sends.at[level, o - 1],
                recv_sem=share_recvs.at[level, o - 1],
                device_id={"core": 1 - core} if level == 0 else peer(axis, o),
                device_id_type=pl.DeviceIdType.MESH,
            )
            copy.start()
            started.append(copy)
            shares[level].append(copy)

    for side in range(2):
        fetch(side, 0)
    pl.semaphore_wait(barrier, len(peers))
    stages = [scatter0, scatter(1), scatter(2), scatter(3), gather(3), gather(2), gather(1), gather0, expand]
    starts = [0] + [1 + 2 * s for s in range(len(stages) - 1)]
    for t in range(chunks + starts[-1]):
        for s in range(len(stages)):
            if 0 <= t - starts[s] < chunks:
                stages[s](t - starts[s])
        if t % 2 == 0 and t // 2 < len(axes):
            share_step(t // 2)
        elif t == 2 * len(axes):
            total_ref[...] = share_sum(len(axes))
    for copy in started:
        copy.wait_send()


def exchange(index, tab, weight, share, sizes):
    own, width = weight.shape[0], weight.shape[-1]
    geo = Geometry(own, sizes)
    chunks = len(geo.plan)
    hops = max(2, *sizes.values()) - 1
    held = [max(n, 16) for n in geo.held]

    def buf(n):
        return pltpu.VMEM((n, 2 * width), jnp.bfloat16)

    vmem = pl.BlockSpec(memory_space=pltpu.VMEM)
    return pl.pallas_call(
        functools.partial(exchange_kernel, own, sizes),
        out_shape=(jax.ShapeDtypeStruct(tab.shape, jnp.float32), jax.ShapeDtypeStruct(share.shape, jnp.float32)),
        in_specs=[pl.BlockSpec(memory_space=pltpu.SMEM), vmem, pl.BlockSpec(memory_space=pl.ANY), vmem],
        out_specs=(vmem, vmem),
        scratch_shapes=[
            buf(2 * geo.modes),
            buf(2 * geo.modes),
            pltpu.VMEM((2 * geo.blocks * max(rows for rows, _ in geo.plan) + PAD, width), jnp.float32),
            pltpu.VMEM(weight.shape, jnp.bfloat16),
            pltpu.VMEM((4,) + share.shape, jnp.float32),
            pltpu.VMEM((4, hops) + share.shape, jnp.float32),
            buf(held[0]), buf(held[1]), buf(held[2]), buf(held[3]),
            buf(held[1]), buf(held[2]), buf(held[3]),
            pltpu.SemaphoreType.DMA((chunks,)),
            pltpu.SemaphoreType.DMA((8, chunks, hops)),
            pltpu.SemaphoreType.DMA((8, chunks, hops)),
            pltpu.SemaphoreType.DMA((4, hops)),
            pltpu.SemaphoreType.DMA((4, hops)),
        ],
        compiler_params=pltpu.CompilerParams(
            collective_id=0, has_side_effects=True, vmem_limit_bytes=35 << 20
        ),
    )(index, tab, weight, share)


def grid_index(mode_table):
    row = lax.broadcasted_iota(jnp.int32, mode_table.shape, 0)
    slot = jnp.where(mode_table >= 0, mode_table, HALF - 1 - mode_table)
    inner = jnp.where(row == 1, (mode_table - KY_LOW) * KZ_COUNT, mode_table - KZ_LOW)
    return jnp.sum(jnp.where(row == 0, slot * PLANE, inner), axis=0)


def on_device(features, coords, quad_weight, mode_table, mode_weight, lin_weight, bias):
    sizes = {a: lax.axis_size(a) for a in ("x", "modes", "z")}
    rows = features.shape[0] // sizes["modes"]
    start = lax.axis_index("modes") * rows
    features = lax.dynamic_slice_in_dim(features, start, rows, 0)
    table = jnp.concatenate([coords, quad_weight[None, :]], axis=0)
    table = lax.dynamic_slice_in_dim(table, start, rows, 1)
    index = 2 * grid_index(mode_table)
    e, tab, xt, share = analyse(table, features, index)
    full, total = exchange(index, tab, mode_weight, share, sizes)
    return synthesize(index, e, xt, full, features, lin_weight, bias, total)


def solution(mesh):
    chips = mesh.shape["pts"] // 2
    n_x = 2 if chips % 2 == 0 else 1
    shape = (chips // n_x, n_x, 2, mesh.shape["modes"])
    mesh = Mesh(mesh.devices.reshape(shape), AXES)
    return jax.shard_map(
        on_device,
        mesh=mesh,
        in_specs=(
            P(PTS, None),
            P(None, PTS),
            P(PTS),
            P(),
            P(AXES, None, None, None),
            P(),
            P(),
        ),
        out_specs=P(AXES, None),
        check_vma=False,
    )
```
